32 devices in a mesh: ctx: 4 (over z), tp: 8 (over y, x, core).
Axes of the slice: x: 2, y: 2, z: 4, core: 2. Of those that a mesh axis runs over, the one named last changes fastest.
Arguments:
- tokens: bfloat16 [512, 8192], P('ctx', 'tp'), may hold values from -6 to 6
- inner_weight: bfloat16 [8192, 8192], P(None, 'tp'), may hold values from -0.0625 to 0.0625
- gate_weight: bfloat16 [8192, 8192], P(None, 'tp'), may hold values from -0.0625 to 0.0625
- conv_weight: float32 [4, 8192], P(None, 'tp'), may hold values from -3 to 3
- conv_bias: float32 [8192], P('tp'), may hold values from -3 to 3
- proj_weight: bfloat16 [8192, 544], P('tp'), may hold values from -0.0625 to 0.0625
- step_weight: bfloat16 [512, 8192], P(None, 'tp'), may hold values from -0.25 to 0.25
- step_bias: float32 [8192], P('tp'), may hold values from -4 to -0.5
- decay_rate: float32 [8192, 16], P('tp'), may hold values from 1e-05 to 2
- skip_gain: float32 [8192], P('tp'), may hold values from -1 to 2
- out_weight: bfloat16 [8192, 8192], P('tp'), may hold values from -0.09375 to 0.09375
- carried_state: float32 [8192, 16], P('tp'), may hold values from -6 to 6
Outputs:
- mixed: bfloat16 [512, 8192], P('ctx', 'tp')
- boundary_states: float32 [4, 8192, 16], P('ctx', 'tp')
The draws below stay inside these ranges and needn't reach their ends.
All inputs are finite; a program needn't handle non-finite values.
Results may differ from the reference program's by a relative error of at most 0.025.
Values may be sent and summed in bfloat16 or wider, within the bound.
No kernel may reach another device: no remote copies, remote signals or barrier semaphores. Data moves between devices by JAX's collectives and lax.ppermute only.
A program may use at most 192 MiB of HBM per device.

```python
import jax
import jax.numpy as jnp
from jax import lax

D = 8192
STATE = 16
CONV = 4
DT_RANK = 512
INNER = 8192
L_DEV = 128
TOKENS = 512
N_CTX = 4
N_TP = 8


def quick_channels(key):
    return jax.random.uniform(jax.random.fold_in(key, 11), (INNER,), jnp.float32) < 0.4


def draw_step_bias(key, part):
    quick = quick_channels(key)
    spread = jax.random.uniform(jax.random.fold_in(key, 12), (INNER,), jnp.float32)
    quick_value = -1.5 + spread
    slow_value = -4.0 + 2.5 * spread
    return jnp.where(quick, quick_value, slow_value).astype(jnp.float32)


def draw_decay_rate(key, part):
    quick = quick_channels(key)[:, None]
    spread = jax.random.uniform(jax.random.fold_in(key, 13), (INNER, STATE), jnp.float32)
    low_log = jnp.log(jnp.float32(1e-05))
    high_log = jnp.log(jnp.float32(2.0))
    slow_value = jnp.exp(low_log + spread * (high_log - low_log))
    quick_value = jnp.exp(jnp.log(jnp.float32(0.5)) + spread * jnp.log(jnp.float32(4.0)))
    return jnp.clip(jnp.where(quick, quick_value, slow_value), 1e-05, 2.0).astype(jnp.float32)


def with_spikes(values, rng, source, target, parts, factor):
    def block_of(position):
        return (jnp.arange(values.shape[position]) // (values.shape[position] // parts)).reshape((-1,) + (1,) * (values.ndim - 1 - position))

    first = jax.random.permutation(rng, parts)[block_of(target)]
    far = (block_of(target) + parts // 2) % parts
    return jnp.where((block_of(source) == first) | (block_of(source) == far), factor * values, values)


def shard_levels(stream_key, shape, cuts, least, top_value):
    level = 1.0
    for position, parts in cuts:
        draws = jax.random.uniform(jax.random.fold_in(jax.random.fold_in(stream_key, 6), position), (parts,), jnp.float32, least / len(cuts), top_value / len(cuts))
        level = level * jnp.repeat(jnp.exp(draws), shape[position] // parts).reshape((-1,) + (1,) * (len(shape) - 1 - position))
    return level


def scatter_about(key, shape, scale, bound, shards=(), held_as=jnp.bfloat16):
    level = shard_levels(key, shape, shards, -0.22, 0.18) if shards else 1.0
    entries = jax.random.normal(key, shape, jnp.float32) * scale * level
    return jnp.minimum(jnp.maximum(entries, -bound), bound).astype(held_as)


def gaussian_with(rng, extent, width, most, shards, heavy, kind=jnp.bfloat16):
    result = width * jax.random.normal(rng, extent, jnp.float32)
    if shards:
        result = result * shard_levels(rng, extent, shards, -0.22, 0.18)
    return jnp.clip(with_spikes(result, jax.random.fold_in(rng, 3), *heavy), -most, most).astype(kind)


def setup_inputs(seed: int = 0) -> dict:
    arg_keys = jax.random.split(jax.random.key(seed), 13)
    tokens = scatter_about(arg_keys[0], (TOKENS, D), 1.0, 6.0, ((0, 4), (1, 8)))
    inner_weight = scatter_about(arg_keys[1], (D, INNER), D ** -0.5, 0.0625, ((1, 8),))
    gate_weight = scatter_about(arg_keys[2], (D, INNER), D ** -0.5, 0.0625, ((1, 8),))
    conv_weight = scatter_about(arg_keys[3], (CONV, INNER), CONV ** -0.5, 3.0, ((1, 8),), jnp.float32)
    conv_bias = scatter_about(arg_keys[4], (INNER,), 0.5, 3.0, ((0, 8),), jnp.float32)
    proj_weight = scatter_about(arg_keys[5], (INNER, DT_RANK + 2 * STATE), INNER ** -0.5, 0.0625, ((0, 8),))
    step_weight = scatter_about(arg_keys[6], (DT_RANK, INNER), DT_RANK ** -0.5, 0.25, ((1, 8),))
    step_bias = draw_step_bias(jax.random.fold_in(arg_keys[12], 71), 0)
    decay_rate = draw_decay_rate(jax.random.fold_in(arg_keys[12], 71), 0)
    skip_gain = jnp.clip(-1.0 + 3.0 * jax.random.uniform(arg_keys[9], (INNER,), jnp.float32) ** shard_levels(arg_keys[9], (INNER,), ((0, 8),), -0.2, 0.2), -1.0, 2.0)
    out_weight = gaussian_with(arg_keys[10], (INNER, D), INNER ** -0.5, 0.09375, ((0, 8),), (0, 1, 8, 2.0))
    carried_state = scatter_about(arg_keys[11], (INNER, STATE), 1.0, 6.0, ((0, 8),), jnp.float32)
    return {"tokens": tokens, "inner_weight": inner_weight, "gate_weight": gate_weight, "conv_weight": conv_weight, "conv_bias": conv_bias, "proj_weight": proj_weight, "step_weight": step_weight, "step_bias": step_bias, "decay_rate": decay_rate, "skip_gain": skip_gain, "out_weight": out_weight, "carried_state": carried_state}


def conv_inner(inner_x, conv_weight, conv_bias, count):
    kernel = conv_weight.shape[0]
    leading_rows = jnp.zeros((kernel - 1, inner_x.shape[1]), jnp.float32)
    padded = jnp.concatenate([leading_rows, inner_x.astype(jnp.float32)], axis=0)
    summed = jnp.broadcast_to(conv_bias[None, :], (count, conv_bias.shape[0]))
    for offset in range(kernel):
        summed = summed + conv_weight[offset][None, :] * padded[offset:offset + count]
    return jax.nn.silu(summed).astype(jnp.bfloat16)


def reference(tokens, inner_weight, gate_weight, conv_weight, conv_bias, proj_weight, step_weight, step_bias, decay_rate, skip_gain, out_weight, carried_state):
    inner_x = jnp.dot(tokens, inner_weight, preferred_element_type=jnp.float32).astype(jnp.bfloat16)
    gate = jnp.dot(tokens, gate_weight, preferred_element_type=jnp.float32).astype(jnp.bfloat16)
    conv_x = conv_inner(inner_x, conv_weight, conv_bias, TOKENS)
    proj = jnp.dot(conv_x, proj_weight, preferred_element_type=jnp.float32)
    low = proj[:, :DT_RANK].astype(jnp.bfloat16)
    step = jax.nn.softplus(jnp.dot(low, step_weight, preferred_element_type=jnp.float32) + step_bias[None, :])
    b_in = proj[:, DT_RANK:DT_RANK + STATE]
    c_out = proj[:, DT_RANK + STATE:]
    conv_float = conv_x.astype(jnp.float32)

    def token_step(hidden, inputs):
        step_row, b_row, c_row, x_row = inputs
        hidden = jnp.exp(-step_row[:, None] * decay_rate) * hidden + (step_row * x_row)[:, None] * b_row[None, :]
        return hidden, jnp.sum(hidden * c_row[None, :], axis=1)

    def shard_step(hidden, inputs):
        hidden, readout = lax.scan(token_step, hidden, inputs)
        return hidden, (readout, hidden)

    shaped = tuple(v.reshape((N_CTX, L_DEV) + v.shape[1:]) for v in (step, b_in, c_out, conv_float))
    final_state, (readout, boundary_states) = lax.scan(shard_step, carried_state.astype(jnp.float32), shaped)
    readout = readout.reshape(TOKENS, INNER)
    gated = ((readout + skip_gain[None, :] * conv_float) * jax.nn.silu(gate.astype(jnp.float32))).astype(jnp.bfloat16)
    block = INNER // N_TP
    gated_blocks = jnp.transpose(gated.reshape(TOKENS, N_TP, block), (1, 0, 2))
    weight_blocks = out_weight.reshape(N_TP, block, D)

    def add_block(total, pair):
        gated_part, weight_part = pair
        partial_value = jnp.dot(gated_part, weight_part, preferred_element_type=jnp.float32).astype(jnp.bfloat16)
        return total + partial_value.astype(jnp.float32), None

    total, unused = lax.scan(add_block, jnp.zeros((TOKENS, D), jnp.float32), (gated_blocks, weight_blocks))
    mixed = total.astype(jnp.bfloat16)
    return mixed, boundary_states
```

```python
import functools

import jax
import jax.numpy as jnp
from jax import lax
from jax.experimental import pallas as pl
from jax.experimental.pallas import tpu as pltpu
from jax.sharding import PartitionSpec as P

STATE = 16
DT_RANK = 512
LANES = 128
F32 = jnp.float32
BF16 = jnp.bfloat16
VMEM = pltpu.VMEM


def flip(value, axis, mask, pairs=None):
    peers = lax.axis_size(axis)
    return lax.ppermute(value, axis, [(i, i ^ mask) for i in range(peers)])


def cost(flops, nbytes, trans=0):
    return pl.CostEstimate(flops=flops, bytes_accessed=nbytes, transcendentals=trans)


def whole(shape):
    zeros = (0,) * len(shape)
    return pl.BlockSpec(shape, lambda *_: zeros)


def mm_kernel(masks, n_w, has_acc, final, tile, me_ref, *refs):
    n_b = len(masks)
    lhs = refs[:n_b]
    w = refs[n_b : n_b + n_w]
    refs = refs[n_b + n_w :]
    acc_in = refs[:n_w] if has_acc else None
    refs = refs[n_w:] if has_acc else refs
    outs = refs[:n_w]
    acc = refs[n_w:] if final else outs
    k = pl.program_id(0)
    j = pl.program_id(1)
    cols = pl.ds(pl.multiple_of(j * tile, tile), tile)
    for i in range(n_b):

        @pl.when(k == i)
        def _(i=i):
            for q in range(n_w):
                part = jnp.dot(lhs[i][...], w[q][...], preferred_element_type=F32)
                if i == 0:
                    if has_acc:
                        part = part + acc_in[q][:, cols]
                else:
                    part = part + acc[q][:, cols]
                if final and i == n_b - 1:
                    outs[q][:, cols] = part.astype(outs[q].dtype)
                else:
                    acc[q][:, cols] = part


def mm(me, blocks, masks, weights, accs, final):
    rows, feat = blocks[0].shape
    ch = weights[0].shape[1]
    tile = min(ch, 512)
    n_w = len(weights)
    has_acc = accs is not None
    wspec = pl.BlockSpec((feat, tile), lambda k, j, me: (me[0] ^ pick(k, masks), j))
    full = whole((rows, ch))
    odt = BF16 if final else F32
    out = pl.pallas_call(
        functools.partial(mm_kernel, masks, n_w, has_acc, final, tile),
        grid_spec=pltpu.PrefetchScalarGridSpec(
            num_scalar_prefetch=1,
            grid=(len(blocks), ch // tile),
            in_specs=[whole((rows, feat))] * len(blocks)
            + [wspec] * n_w
            + ([full] * n_w if has_acc else []),
            out_specs=[full] * n_w,
            scratch_shapes=[VMEM((rows, ch), F32)] * (n_w if final else 0),
        ),
        out_shape=[jax.ShapeDtypeStruct((rows, ch), odt)] * n_w,
        cost_estimate=cost(
            2 * rows * feat * len(blocks) * ch * n_w, 2 * feat * len(blocks) * ch * n_w
        ),
    )(me, *blocks, *weights, *(accs or ()))
    return out


def pick(k, values):
    result = values[0]
    for i in range(1, len(values)):
        result = jnp.where(k == i, values[i], result)
    return result


def conv_kernel(split, core_ref, x_ref, tail_ref, w_ref, b_ref, pw_ref, conv_ref, send_ref, keep_ref, pad, acc):
    rows, ch = x_ref.shape
    taps = w_ref.shape[0]
    edge = tail_ref.shape[0]
    pad[0:edge, :] = tail_ref[...].astype(F32)
    pad[edge : edge + rows, :] = x_ref[...].astype(F32)
    total = jnp.broadcast_to(b_ref[...], (rows, ch))
    for k in range(taps):
        total = total + w_ref[k : k + 1, :] * pad[edge - taps + 1 + k : edge - taps + 1 + k + rows, :]
    conv = (total * jax.nn.sigmoid(total)).astype(BF16)
    conv_ref[...] = conv
    proj = lax.dot_general(conv, pw_ref[...], (((1,), (1,)), ((), ())), preferred_element_type=F32)
    if split:
        half = rows // 2
        core = core_ref[0]
        acc[...] = proj
        send_ref[...] = acc[pl.ds(pl.multiple_of((1 - core) * half, half), half), :].astype(BF16)
        keep_ref[...] = acc[pl.ds(pl.multiple_of(core * half, half), half), :]
    else:
        keep_ref[...] = proj.astype(keep_ref.dtype)
        send_ref[...] = jnp.zeros(send_ref.shape, send_ref.dtype)


def conv_proj(core, x, tail, conv_w, conv_b, proj_wt, split):
    rows, ch = x.shape
    wide = proj_wt.shape[0]
    half = rows // 2 if split else rows
    shalf = half if split else 8
    return pl.pallas_call(
        functools.partial(conv_kernel, split),
        in_specs=[pl.BlockSpec(memory_space=pltpu.SMEM)] + [pl.BlockSpec(memory_space=VMEM)] * 5,
        out_specs=[pl.BlockSpec(memory_space=VMEM)] * 3,
        out_shape=[
            jax.ShapeDtypeStruct((rows, ch), BF16),
            jax.ShapeDtypeStruct((shalf, wide), BF16),
            jax.ShapeDtypeStruct((half, wide), F32 if split else BF16),
        ],
        scratch_shapes=[VMEM((tail.shape[0] + rows, ch), F32), VMEM((rows, wide), F32)],
        cost_estimate=cost(2 * rows * ch * wide, 2 * ch * wide),
    )(core, x, tail, conv_w, conv_b, proj_wt)


def spread(ref, value, groups):
    count = value.shape[0]
    for j in range(groups):
        ref[pl.ds(j, count, stride=groups), :] = value[:, j * LANES : (j + 1) * LANES]


def collect(ref, count, groups):
    return jnp.concatenate([ref[pl.ds(j, count, stride=groups), :] for j in range(groups)], axis=1)


def scan_kernel(
    lead_ref, bc_ref, low_ref, conv_ref, sw_ref, sb_ref, decay_ref, carried_ref,
    end_ref, y_ref, cum_ref,
    step_s, drive_s, nd_s, h_s,
):
    rows, ch = conv_ref.shape
    groups = ch // LANES
    pre = jnp.dot(low_ref[...], sw_ref[...], preferred_element_type=F32) + sb_ref[...]
    step = jnp.maximum(pre, 0.0) + jnp.log1p(jnp.exp(-jnp.abs(pre)))
    spread(step_s, step, groups)
    spread(drive_s, step * conv_ref[...].astype(F32), groups)
    spread(nd_s, -decay_ref[...], groups)
    spread(h_s, carried_ref[...] * lead_ref[0], groups)
    nd = [nd_s[n * groups : (n + 1) * groups, :] for n in range(STATE)]
    h0 = tuple(h_s[n * groups : (n + 1) * groups, :] for n in range(STATE))

    def body(t, carry):
        h, total = carry
        at = pl.ds(pl.multiple_of(t * groups, groups), groups)
        dt = step_s[at, :]
        u = drive_s[at, :]
        total = total + dt
        cum_ref[at, :] = total
        y = None
        new = []
        for n in range(STATE):
            a = jnp.exp(dt * nd[n])
            v = a * h[n] + u * bc_ref[t, n]
            new.append(v)
            term = v * bc_ref[t, STATE + n]
            y = term if y is None else y + term
        y_ref[at, :] = y
        return tuple(new), total

    h, total = lax.fori_loop(0, rows, body, (h0, jnp.zeros((groups, LANES), F32)), unroll=4)
    for n in range(STATE):
        h_s[n * groups : (n + 1) * groups, :] = h[n]
    end_ref[0:STATE, :] = collect(h_s, STATE, groups)
    nd_s[0:groups, :] = total
    end_ref[STATE : STATE + 1, :] = collect(nd_s, 1, groups)


def scan(lead, bc, low, conv_x, step_w, step_b, decay_t, carried_t):
    rows, ch = conv_x.shape
    groups = ch // LANES
    vm = pl.BlockSpec(memory_space=VMEM)
    sm = pl.BlockSpec(memory_space=pltpu.SMEM)
    return pl.pallas_call(
        scan_kernel,
        in_specs=[sm, sm] + [vm] * 6,
        out_specs=[vm] * 3,
        out_shape=[
            jax.ShapeDtypeStruct((STATE + 1, ch), F32),
            jax.ShapeDtypeStruct((rows * groups, LANES), F32),
            jax.ShapeDtypeStruct((rows * groups, LANES), F32),
        ],
        scratch_shapes=[
            VMEM((rows * groups, LANES), F32),
            VMEM((rows * groups, LANES), F32),
            VMEM((STATE * groups, LANES), F32),
            VMEM((STATE * groups, LANES), F32),
        ],
        cost_estimate=cost(rows * ch * STATE * 8, rows * ch * 8, rows * ch * STATE),
    )(lead, bc, low, conv_x, step_w, step_b, decay_t, carried_t)


def gate_kernel(bc_ref, y_ref, cum_ref, enter_ref, decay_ref, conv_ref, skip_ref, gate_ref, out_ref, nd_s, e_s, y_s):
    rows, ch = conv_ref.shape
    groups = ch // LANES
    spread(nd_s, -decay_ref[...], groups)
    spread(e_s, enter_ref[...], groups)
    nd = [nd_s[n * groups : (n + 1) * groups, :] for n in range(STATE)]
    ent = [e_s[n * groups : (n + 1) * groups, :] for n in range(STATE)]

    def body(t, carry):
        at = pl.ds(pl.multiple_of(t * groups, groups), groups)
        total = cum_ref[at, :]
        y = y_ref[at, :]
        for n in range(STATE):
            y = y + jnp.exp(total * nd[n]) * ent[n] * bc_ref[t, STATE + n]
        y_s[at, :] = y
        return carry

    lax.fori_loop(0, rows, body, 0, unroll=4)
    y = collect(y_s, rows, groups)
    gate = gate_ref[...].astype(F32)
    out = (y + skip_ref[...] * conv_ref[...].astype(F32)) * (gate * jax.nn.sigmoid(gate))
    out_ref[...] = out.astype(BF16)


def gating(bc, y, cum, entering, decay_t, conv_x, skip, gate):
    rows, ch = conv_x.shape
    groups = ch // LANES
    vm = pl.BlockSpec(memory_space=VMEM)
    sm = pl.BlockSpec(memory_space=pltpu.SMEM)
    return pl.pallas_call(
        gate_kernel,
        in_specs=[sm] + [vm] * 7,
        out_specs=vm,
        out_shape=jax.ShapeDtypeStruct((rows, ch), BF16),
        scratch_shapes=[
            VMEM((STATE * groups, LANES), F32),
            VMEM((STATE * groups, LANES), F32),
            VMEM((rows * groups, LANES), F32),
        ],
        cost_estimate=cost(rows * ch * STATE * 6, rows * ch * 8, rows * ch * STATE),
    )(bc, y, cum, entering, decay_t, conv_x, skip, gate)


def out_kernel(me_ref, g_ref, w_ref, o_ref):
    o_ref[0] = jnp.dot(g_ref[...], w_ref[...], preferred_element_type=F32).astype(o_ref.dtype)


def out_blocks(me, gated, weight, masks, feat, dtype):
    rows, ch = gated.shape
    tile = min(feat, 512)
    per = feat // tile
    return pl.pallas_call(
        out_kernel,
        grid_spec=pltpu.PrefetchScalarGridSpec(
            num_scalar_prefetch=1,
            grid=(len(masks), per),
            in_specs=[
                whole((rows, ch)),
                pl.BlockSpec((ch, tile), lambda k, j, me: (0, (me[0] ^ pick(k, masks)) * per + j)),
            ],
            out_specs=pl.BlockSpec((1, rows, tile), lambda k, j, me: (k, 0, j)),
        ),
        out_shape=jax.ShapeDtypeStruct((len(masks), rows, feat), dtype),
        cost_estimate=cost(2 * rows * ch * feat * len(masks), 2 * ch * feat * len(masks)),
    )(me, gated, weight)


def on_device(
    tokens, inner_weight, gate_weight, conv_weight, conv_bias, proj_weight, step_weight,
    step_bias, decay_rate, skip_gain, out_weight, carried_state,
):
    rows, feat = tokens.shape
    taps = conv_weight.shape[0]
    n_tp = lax.axis_size("tp")
    n_ctx = lax.axis_size("ctx")
    tp = lax.axis_index("tp")
    ctx = lax.axis_index("ctx")
    me = tp.astype(jnp.int32).reshape(1)
    core = tp % 2
    core1 = core.astype(jnp.int32).reshape(1)
    square = n_tp == 8

    if square:
        px = flip(tokens, "tp", 2)
        py = flip(tokens, "tp", 4)
        pd = flip(tokens, "tp", 6)
        p1 = flip(tokens, "tp", 1)
        both = [inner_weight, gate_weight]
        acc = mm(me, [tokens, p1], [0, 1], both, None, False)
        qx = flip(px, "tp", 1)
        qy = flip(py, "tp", 1)
        qd = flip(pd, "tp", 1)
        acc = mm(me, [px, qx], [2, 3], both, acc, False)
        acc = mm(me, [py, qy], [4, 5], both, acc, False)
        (inner_x,) = mm(me, [pd, qd], [6, 7], [inner_weight], [acc[0]], True)
        (gate,) = mm(me, [pd, qd], [6, 7], [gate_weight], [acc[1]], True)
    else:
        piece = lax.all_gather(tokens, "tp", axis=1, tiled=True)
        inner_x = jnp.dot(piece, inner_weight, preferred_element_type=F32).astype(BF16)
        gate = jnp.dot(piece, gate_weight, preferred_element_type=F32).astype(BF16)

    edge = 8
    tail = lax.ppermute(
        inner_x[rows - edge :], "ctx", [(i, i + 1) for i in range(n_ctx - 1)]
    )
    conv_x, send, keep = conv_proj(
        core1, inner_x, tail, conv_weight, conv_bias[None, :], proj_weight.T, square
    )
    if square:
        part = (keep + flip(send, "tp", 1).astype(F32)).astype(BF16)
        quarter = [flip(part, "tp", m).astype(F32) for m in (2, 4, 6)]
        mine = (part.astype(F32) + quarter[0] + (quarter[1] + quarter[2])).astype(BF16)
        other = flip(mine, "tp", 1)
        first = jnp.where(core == 0, mine, other)
        second = jnp.where(core == 0, other, mine)
        proj = jnp.concatenate([first, second], axis=0)
    else:
        proj = lax.psum(keep, "tp")
    low = proj[:, :DT_RANK]
    bc = proj[:, DT_RANK:].astype(F32)

    decay_t = jnp.transpose(decay_rate)
    carried_t = jnp.transpose(carried_state)
    leading = ctx == 0
    lead = leading.astype(F32).reshape(1)
    end, y, cum = scan(
        lead, bc, low, conv_x, step_weight, step_bias[None, :], decay_t, carried_t
    )

    group = end
    entering = jnp.zeros_like(end[:STATE])
    before = jnp.zeros_like(end[STATE:])
    bit = 1
    while bit < n_ctx:
        last = bit * 2 >= n_ctx
        upper = (ctx & bit) != 0
        if last:
            pairs = [(i, i ^ bit) for i in range(n_ctx) if not i & bit]
            got = lax.ppermute(group[:STATE], "ctx", pairs)
            entering = jnp.where(upper, jnp.exp(-decay_t * before) * got + entering, entering)
        else:
            got = flip(group, "ctx", bit)
            gs, gh = got[STATE:], got[:STATE]
            ms, mh = group[STATE:], group[:STATE]
            entering = jnp.where(upper, jnp.exp(-decay_t * before) * gh + entering, entering)
            before = jnp.where(upper, before + gs, before)
            total = jnp.where(
                upper, jnp.exp(-decay_t * ms) * gh + mh, jnp.exp(-decay_t * gs) * mh + gh
            )
            group = jnp.concatenate([total, ms + gs], axis=0)
        bit *= 2
    boundary = jnp.transpose(jnp.exp(-decay_t * end[STATE:]) * entering + end[:STATE])[None]

    gated = gating(bc, y, cum, entering, decay_t, conv_x, skip_gain[None, :], gate)
    if square:
        away = out_blocks(me, gated, out_weight, [7, 3, 5, 1], feat, BF16)
        got = flip(away, "tp", 1)
        near = out_blocks(me, gated, out_weight, [6, 2, 4, 0], feat, BF16)
        chip = (near.astype(F32) + got.astype(F32)).astype(BF16)
        rd = flip(chip[0], "tp", 6)
        rx = flip(chip[1], "tp", 2)
        ry = flip(chip[2], "tp", 4)
        mixed = (
            (chip[3].astype(F32) + rx.astype(F32)) + (ry.astype(F32) + rd.astype(F32))
        ).astype(BF16)
    else:
        partial = jnp.dot(gated, out_weight, preferred_element_type=F32).astype(BF16)
        mixed = lax.psum_scatter(partial, "tp", scatter_dimension=1, tiled=True)
    return (mixed, boundary)


def solution(mesh):
    in_specs = (
        P("ctx", "tp"), P(None, "tp"), P(None, "tp"), P(None, "tp"), P("tp"), P("tp", None),
        P(None, "tp"), P("tp"), P("tp", None), P("tp"), P("tp", None), P("tp", None),
    )
    out_specs = (P("ctx", "tp"), P("ctx", "tp", None))
    return jax.shard_map(
        on_device, mesh=mesh, in_specs=in_specs, out_specs=out_specs, check_vma=False
    )
```

```python
import functools

import jax
import jax.numpy as jnp
from jax import lax
from jax.experimental import pallas as pl
from jax.experimental.pallas import tpu as pltpu
from jax.sharding import PartitionSpec as P

STATE = 16
DT_RANK = 512
LANES = 128
EDGE = 8
F32 = jnp.float32
BF16 = jnp.bfloat16
VMEM = pltpu.VMEM


def flip(value, axis, mask, pairs=None):
    peers = lax.axis_size(axis)
    return lax.ppermute(value, axis, [(i, i ^ mask) for i in range(peers)])


def cost(flops, nbytes, trans=0):
    return pl.CostEstimate(flops=flops, bytes_accessed=nbytes, transcendentals=trans)


def whole(shape):
    zeros = (0,) * len(shape)
    return pl.BlockSpec(shape, lambda *_: zeros)


PIECES = 2


def params(mib):
    return pltpu.CompilerParams(vmem_limit_bytes=mib << 20)


def far(value):
    return pltpu.with_memory_space_constraint(value, pltpu.HBM)


def tie(value, *others):
    return lax.optimization_barrier((value, *others))[0]


def row_copies(masks, weights, bufs, sem, feat):
    copies = []
    piece = feat // PIECES
    for q, (w, buf) in enumerate(zip(weights, bufs)):
        for i, mask in enumerate(masks):
            for p in range(PIECES):
                at = pl.multiple_of((lax.axis_index("tp") ^ mask) * feat + p * piece, piece)
                copies.append(
                    pltpu.make_async_copy(
                        w.at[pl.ds(at, piece), :],
                        buf.at[pl.ds(i * feat + p * piece, piece), :],
                        sem.at[(q * len(masks) + i) * PIECES + p],
                    )
                )
    return copies


def mm_kernel(masks, n_w, has_acc, *refs):
    n_b = len(masks)
    lhs = refs[:n_b]
    w = refs[n_b : n_b + n_w]
    refs = refs[n_b + n_w :]
    acc_in = refs[:n_w] if has_acc else None
    refs = refs[n_w:] if has_acc else refs
    outs = refs[:n_w]
    bufs = refs[n_w : 2 * n_w]
    sem = refs[2 * n_w]
    feat = lhs[0].shape[1]
    piece = feat // PIECES
    copies = row_copies(masks, w, bufs, sem, feat)
    for c in copies:
        c.start()
    step = 0
    for q in range(n_w):
        total = acc_in[q][...] if has_acc else None
        for i in range(n_b):
            for p in range(PIECES):
                copies[step].wait()
                step += 1
                part = jnp.dot(
                    lhs[i][:, p * piece : (p + 1) * piece],
                    bufs[q][i * feat + p * piece : i * feat + (p + 1) * piece, :],
                    preferred_element_type=F32,
                )
                total = part if total is None else total + part
        outs[q][...] = total


def mm(blocks, masks, weights, accs):
    rows, feat = blocks[0].shape
    ch = weights[0].shape[1]
    n_w = len(weights)
    has_acc = accs is not None
    vm = pl.BlockSpec(memory_space=VMEM)
    depth = feat * len(blocks)
    return pl.pallas_call(
        functools.partial(mm_kernel, masks, n_w, has_acc),
        in_specs=[vm] * len(blocks)
        + [pl.BlockSpec(memory_space=pltpu.HBM)] * n_w
        + [vm] * (n_w if has_acc else 0),
        out_specs=[vm] * n_w,
        out_shape=[jax.ShapeDtypeStruct((rows, ch), F32)] * n_w,
        scratch_shapes=[VMEM((depth, ch), BF16)] * n_w
        + [pltpu.SemaphoreType.DMA((n_w * len(blocks) * PIECES,))],
        compiler_params=params(12),
        cost_estimate=cost(2 * rows * depth * ch * n_w, 2 * depth * ch * n_w),
    )(*blocks, *map(far, weights), *(accs or ()))


def fetch_kernel(masks, n_w, *refs):
    w = refs[:n_w]
    outs = refs[n_w : 2 * n_w]
    sem = refs[2 * n_w]
    copies = row_copies(masks, w, outs, sem, outs[0].shape[0] // len(masks))
    for c in copies:
        c.start()
    for c in copies:
        c.wait()


def fetch(masks, weights, feat):
    ch = weights[0].shape[1]
    n_w = len(weights)
    depth = feat * len(masks)
    return pl.pallas_call(
        functools.partial(fetch_kernel, masks, n_w),
        in_specs=[pl.BlockSpec(memory_space=pltpu.HBM)] * n_w,
        out_specs=[pl.BlockSpec(memory_space=VMEM)] * n_w,
        out_shape=[VMEM((depth, ch), BF16)] * n_w,
        scratch_shapes=[pltpu.SemaphoreType.DMA((n_w * len(masks) * PIECES,))],
        compiler_params=params(1),
        cost_estimate=cost(0, 2 * depth * ch * n_w),
    )(*map(far, weights))


def last_kernel(edge, a_ref, b_ref, w_ref, acc_ref, out_ref, edge_ref=None):
    feat = a_ref.shape[1]
    total = acc_ref[...] + jnp.dot(a_ref[...], w_ref[:feat, :], preferred_element_type=F32)
    total = total + jnp.dot(b_ref[...], w_ref[feat:, :], preferred_element_type=F32)
    out_ref[...] = total.astype(BF16)
    if edge:
        edge_ref[...] = total[total.shape[0] - edge :].astype(BF16)


def finish(a, b, w, acc, edge=0):
    rows, feat = a.shape
    ch = w.shape[1]
    vm = pl.BlockSpec(memory_space=VMEM)
    shapes = [jax.ShapeDtypeStruct((rows, ch), BF16)]
    if edge:
        shapes.append(jax.ShapeDtypeStruct((edge, ch), BF16))
    return pl.pallas_call(
        functools.partial(last_kernel, edge),
        in_specs=[vm] * 4,
        out_specs=[vm] * len(shapes),
        out_shape=shapes,
        compiler_params=params(4),
        cost_estimate=cost(4 * rows * feat * ch, 4 * feat * ch),
    )(a, b, pltpu.with_memory_space_constraint(w, VMEM), acc)


def conv_kernel(split, x_ref, tail_ref, w_ref, b_ref, pw_ref, conv_ref, send_ref, keep_ref, pad, acc):
    rows, ch = x_ref.shape
    taps = w_ref.shape[0]
    edge = tail_ref.shape[0]
    pad[0:edge, :] = tail_ref[...].astype(F32)
    pad[edge : edge + rows, :] = x_ref[...].astype(F32)
    total = jnp.broadcast_to(b_ref[...], (rows, ch))
    for k in range(taps):
        total = total + w_ref[k : k + 1, :] * pad[edge - taps + 1 + k : edge - taps + 1 + k + rows, :]
    conv = (total * jax.nn.sigmoid(total)).astype(BF16)
    conv_ref[...] = conv
    proj = lax.dot_general(conv, pw_ref[...], (((1,), (1,)), ((), ())), preferred_element_type=F32)
    if split:
        half = rows // 2
        core = lax.axis_index("tp") % 2
        acc[...] = proj
        send_ref[...] = acc[pl.ds(pl.multiple_of((1 - core) * half, half), half), :].astype(BF16)
        keep_ref[...] = acc[pl.ds(pl.multiple_of(core * half, half), half), :]
    else:
        keep_ref[...] = proj.astype(keep_ref.dtype)
        send_ref[...] = jnp.zeros(send_ref.shape, send_ref.dtype)


def conv_proj(x, tail, conv_w, conv_b, proj_wt, split):
    rows, ch = x.shape
    wide = proj_wt.shape[0]
    half = rows // 2 if split else rows
    shalf = half if split else 8
    return pl.pallas_call(
        functools.partial(conv_kernel, split),
        in_specs=[pl.BlockSpec(memory_space=VMEM)] * 5,
        out_specs=[pl.BlockSpec(memory_space=VMEM)] * 3,
        out_shape=[
            jax.ShapeDtypeStruct((rows, ch), BF16),
            jax.ShapeDtypeStruct((shalf, wide), BF16),
            jax.ShapeDtypeStruct((half, wide), F32 if split else BF16),
        ],
        scratch_shapes=[VMEM((tail.shape[0] + rows, ch), F32), VMEM((rows, wide), F32)],
        compiler_params=params(6),
        cost_estimate=cost(2 * rows * ch * wide, 2 * ch * wide),
    )(x, tail, conv_w, conv_b, proj_wt)


def spread(ref, value, groups):
    count = value.shape[0]
    for j in range(groups):
        ref[pl.ds(j, count, stride=groups), :] = value[:, j * LANES : (j + 1) * LANES]


def collect(ref, count, groups):
    return jnp.concatenate([ref[pl.ds(j, count, stride=groups), :] for j in range(groups)], axis=1)


def to_smem(bc_v, bc_s, sem):
    copy = pltpu.make_async_copy(bc_v, bc_s, sem)
    copy.start()
    return copy


def scan_kernel(
    split, *refs,
):
    n_p = 2 if split else 1
    parts = refs[:n_p]
    (conv_ref, sw_ref, sb_ref, decay_ref, carried_ref,
     end_ref, y_ref, cum_ref, bc_ref,
     proj_s, step_s, drive_s, nd_s, h_s, bc_s, sem) = refs[n_p:]
    rows, ch = conv_ref.shape
    groups = ch // LANES
    if split:
        half = rows // 2
        core = lax.axis_index("tp") % 2
        proj_s[pl.ds(pl.multiple_of(core * half, half), half), :] = parts[0][...].astype(F32)
        proj_s[pl.ds(pl.multiple_of((1 - core) * half, half), half), :] = parts[1][...].astype(F32)
    else:
        proj_s[...] = parts[0][...].astype(F32)
    bc_ref[:, : 2 * STATE] = proj_s[:, DT_RANK:]
    copy = to_smem(bc_ref, bc_s, sem)
    low = proj_s[:, :DT_RANK].astype(BF16)
    pre = jnp.dot(low, sw_ref[...], preferred_element_type=F32) + sb_ref[...]
    step = jnp.maximum(pre, 0.0) + jnp.log1p(jnp.exp(-jnp.abs(pre)))
    spread(step_s, step, groups)
    spread(drive_s, step * conv_ref[...].astype(F32), groups)
    spread(nd_s, -decay_ref[...], groups)
    lead = jnp.where(lax.axis_index("ctx") == 0, 1.0, 0.0)
    spread(h_s, carried_ref[...] * lead, groups)
    nd = [nd_s[n * groups : (n + 1) * groups, :] for n in range(STATE)]
    h0 = tuple(h_s[n * groups : (n + 1) * groups, :] for n in range(STATE))
    copy.wait()

    def body(t, carry):
        h, total = carry
        at = pl.ds(pl.multiple_of(t * groups, groups), groups)
        dt = step_s[at, :]
        u = drive_s[at, :]
        total = total + dt
        cum_ref[at, :] = total
        y = None
        new = []
        for n in range(STATE):
            a = jnp.exp(dt * nd[n])
            v = a * h[n] + u * bc_s[t, n]
            new.append(v)
            term = v * bc_s[t, STATE + n]
            y = term if y is None else y + term
        y_ref[at, :] = y
        return tuple(new), total

    h, total = lax.fori_loop(0, rows, body, (h0, jnp.zeros((groups, LANES), F32)), unroll=4)
    for n in range(STATE):
        h_s[n * groups : (n + 1) * groups, :] = h[n]
    end_ref[0:STATE, :] = collect(h_s, STATE, groups)
    nd_s[0:groups, :] = total
    end_ref[STATE : STATE + 1, :] = collect(nd_s, 1, groups)


def scan(parts, conv_x, step_w, step_b, decay_t, carried_t):
    rows, ch = conv_x.shape
    groups = ch // LANES
    vm = pl.BlockSpec(memory_space=VMEM)
    return pl.pallas_call(
        functools.partial(scan_kernel, len(parts) == 2),
        in_specs=[vm] * (5 + len(parts)),
        out_specs=[vm] * 4,
        out_shape=[
            jax.ShapeDtypeStruct((STATE + 1, ch), F32),
            jax.ShapeDtypeStruct((rows * groups, LANES), F32),
            jax.ShapeDtypeStruct((rows * groups, LANES), F32),
            jax.ShapeDtypeStruct((rows, LANES), F32),
        ],
        scratch_shapes=[
            VMEM((rows, parts[0].shape[1]), F32),
            VMEM((rows * groups, LANES), F32),
            VMEM((rows * groups, LANES), F32),
            VMEM((STATE * groups, LANES), F32),
            VMEM((STATE * groups, LANES), F32),
            pltpu.SMEM((rows, LANES), F32),
            pltpu.SemaphoreType.DMA,
        ],
        compiler_params=params(8),
        cost_estimate=cost(rows * ch * STATE * 8, rows * ch * 8, rows * ch * STATE),
    )(*parts, conv_x, step_w, step_b, decay_t, carried_t)


def add_kernel(*refs):
    total = refs[0][...].astype(F32)
    for r in refs[1:-1]:
        total = total + r[...].astype(F32)
    refs[-1][...] = total.astype(BF16)


def add(*values):
    vm = pl.BlockSpec(memory_space=VMEM)
    shape = values[0].shape
    size = shape[0] * shape[1]
    return pl.pallas_call(
        add_kernel,
        in_specs=[vm] * len(values),
        out_specs=vm,
        out_shape=jax.ShapeDtypeStruct(shape, BF16),
        compiler_params=params(3),
        cost_estimate=cost(size * len(values), 2 * size * len(values)),
    )(*values)


def add_pair_kernel(a_ref, b_ref, *outs):
    for i, o in enumerate(outs):
        o[...] = (a_ref[i].astype(F32) + b_ref[i].astype(F32)).astype(BF16)


def add_pair(a, b):
    vm = pl.BlockSpec(memory_space=VMEM)
    n, rows, feat = a.shape
    return pl.pallas_call(
        add_pair_kernel,
        in_specs=[vm, vm],
        out_specs=[vm] * n,
        out_shape=[jax.ShapeDtypeStruct((rows, feat), BF16)] * n,
        compiler_params=params(3),
        cost_estimate=cost(a.size, 6 * a.size),
    )(a, b)


def merge_kernel(bit, first, decay_ref, group_ref, got_ref, *refs):
    ent_ref = None if first else refs[0]
    new_ref, out_ref = refs[-2:]
    upper = (lax.axis_index("ctx") // bit) % 2 == 1
    decay = decay_ref[...]
    gh, gs = got_ref[:STATE, :], got_ref[STATE:, :]
    mh, ms = group_ref[:STATE, :], group_ref[STATE:, :]
    entering = gh if first else jnp.exp(-decay * ent_ref[STATE:, :]) * gh + ent_ref[:STATE, :]
    before = gs if first else ent_ref[STATE:, :] + gs
    keep_h = jnp.zeros_like(gh) if first else ent_ref[:STATE, :]
    keep_s = jnp.zeros_like(gs) if first else ent_ref[STATE:, :]
    out_ref[:STATE, :] = jnp.where(upper, entering, keep_h)
    out_ref[STATE:, :] = jnp.where(upper, before, keep_s)
    low = jnp.where(upper, gh, mh)
    high = jnp.where(upper, mh, gh)
    high_s = jnp.where(upper, ms, gs)
    new_ref[:STATE, :] = jnp.exp(-decay * high_s) * low + high
    new_ref[STATE:, :] = ms + gs


def merge(bit, decay_t, group, got, ent):
    vm = pl.BlockSpec(memory_space=VMEM)
    first = ent is None
    extra = () if first else (ent,)
    return pl.pallas_call(
        functools.partial(merge_kernel, bit, first),
        in_specs=[vm] * (3 + len(extra)),
        out_specs=[vm, vm],
        out_shape=[jax.ShapeDtypeStruct(group.shape, F32)] * 2,
        compiler_params=params(3),
        cost_estimate=cost(group.size * 8, group.size * 16),
    )(decay_t, group, got, *extra)


def gate_kernel(bit, first, y_ref, cum_ref, bc_ref, end_ref, got_ref, decay_ref, conv_ref, skip_ref, gate_ref, *refs):
    ent_ref = None if first else refs[0]
    out_ref, bound_ref, nd_s, e_s, y_s, bc_s, sem = refs[-7:]
    rows, ch = conv_ref.shape
    groups = ch // LANES
    copy = to_smem(bc_ref, bc_s, sem)
    decay = decay_ref[...]
    upper = (lax.axis_index("ctx") // bit) % 2 == 1
    got = got_ref[:STATE, :]
    if first:
        entering = jnp.where(upper, got, jnp.zeros_like(got))
    else:
        kept = ent_ref[:STATE, :]
        entering = jnp.where(upper, jnp.exp(-decay * ent_ref[STATE:, :]) * got + kept, kept)
    bound_ref[...] = jnp.exp(-decay * end_ref[STATE:, :]) * entering + end_ref[:STATE, :]
    spread(nd_s, -decay, groups)
    spread(e_s, entering, groups)
    nd = [nd_s[n * groups : (n + 1) * groups, :] for n in range(STATE)]
    ent = [e_s[n * groups : (n + 1) * groups, :] for n in range(STATE)]
    copy.wait()

    def body(t, carry):
        at = pl.ds(pl.multiple_of(t * groups, groups), groups)
        total = cum_ref[at, :]
        y = y_ref[at, :]
        for n in range(STATE):
            y = y + jnp.exp(total * nd[n]) * ent[n] * bc_s[t, STATE + n]
        y_s[at, :] = y
        return carry

    lax.fori_loop(0, rows, body, 0, unroll=4)
    y = collect(y_s, rows, groups)
    gate = gate_ref[...].astype(BF16).astype(F32)
    out = (y + skip_ref[...] * conv_ref[...].astype(F32)) * (gate * jax.nn.sigmoid(gate))
    out_ref[...] = out.astype(BF16)


def gating(bit, y, cum, bc, end, got, ent, decay_t, conv_x, skip, gate):
    rows, ch = conv_x.shape
    groups = ch // LANES
    vm = pl.BlockSpec(memory_space=VMEM)
    first = ent is None
    extra = () if first else (ent,)
    return pl.pallas_call(
        functools.partial(gate_kernel, bit, first),
        in_specs=[vm] * (9 + len(extra)),
        out_specs=[vm, vm],
        out_shape=[
            jax.ShapeDtypeStruct((rows, ch), BF16),
            jax.ShapeDtypeStruct((STATE, ch), F32),
        ],
        scratch_shapes=[
            VMEM((STATE * groups, LANES), F32),
            VMEM((STATE * groups, LANES), F32),
            VMEM((rows * groups, LANES), F32),
            pltpu.SMEM((rows, LANES), F32),
            pltpu.SemaphoreType.DMA,
        ],
        compiler_params=params(8),
        cost_estimate=cost(rows * ch * STATE * 6, rows * ch * 8, rows * ch * STATE),
    )(y, cum, bc, end, got, decay_t, conv_x, skip, gate, *extra)


def col_copies(masks, w, buf, sem, feat):
    copies = []
    for i, mask in enumerate(masks):
        at = pl.multiple_of((lax.axis_index("tp") ^ mask) * feat, feat)
        copies.append(
            pltpu.make_async_copy(w.at[:, pl.ds(at, feat)], buf.at[i], sem.at[i])
        )
    return copies


def cols_kernel(masks, w_ref, dep_ref, out_ref, sem):
    copies = col_copies(masks, w_ref, out_ref, sem, out_ref.shape[2])
    for c in copies:
        c.start()
    for c in copies:
        c.wait()


def fetch_cols(masks, weight, feat, dep):
    ch = weight.shape[0]
    return pl.pallas_call(
        functools.partial(cols_kernel, masks),
        in_specs=[
            pl.BlockSpec(memory_space=pltpu.HBM),
            pl.BlockSpec(memory_space=VMEM),
        ],
        out_specs=pl.BlockSpec(memory_space=VMEM),
        out_shape=VMEM((len(masks), ch, feat), BF16),
        scratch_shapes=[pltpu.SemaphoreType.DMA((len(masks),))],
        compiler_params=params(1),
        cost_estimate=cost(0, 2 * ch * feat * len(masks)),
    )(far(weight), dep)


def out_held_kernel(g_ref, w_ref, o_ref):
    for i in range(w_ref.shape[0]):
        o_ref[i] = jnp.dot(g_ref[...], w_ref[i], preferred_element_type=F32).astype(o_ref.dtype)


def out_held(gated, cols):
    rows, ch = gated.shape
    n, _, feat = cols.shape
    vm = pl.BlockSpec(memory_space=VMEM)
    return pl.pallas_call(
        out_held_kernel,
        in_specs=[vm, vm],
        out_specs=vm,
        out_shape=jax.ShapeDtypeStruct((n, rows, feat), BF16),
        compiler_params=params(4),
        cost_estimate=cost(2 * rows * ch * feat * n, 2 * ch * feat * n),
    )(gated, pltpu.with_memory_space_constraint(cols, VMEM))


def out_kernel(masks, g_ref, w_ref, o_ref, buf, sem):
    copies = col_copies(masks, w_ref, buf, sem, o_ref.shape[2])
    for c in copies:
        c.start()
    for i, c in enumerate(copies):
        c.wait()
        o_ref[i] = jnp.dot(g_ref[...], buf[i], preferred_element_type=F32).astype(o_ref.dtype)


def out_blocks(gated, weight, masks, feat):
    rows, ch = gated.shape
    n = len(masks)
    vm = pl.BlockSpec(memory_space=VMEM)
    return pl.pallas_call(
        functools.partial(out_kernel, masks),
        in_specs=[vm, pl.BlockSpec(memory_space=pltpu.HBM)],
        out_specs=vm,
        out_shape=jax.ShapeDtypeStruct((n, rows, feat), BF16),
        scratch_shapes=[VMEM((n, ch, feat), BF16), pltpu.SemaphoreType.DMA((n,))],
        compiler_params=params(12),
        cost_estimate=cost(2 * rows * ch * feat * n, 2 * ch * feat * n),
    )(gated, far(weight))


def on_device(
    tokens, inner_weight, gate_weight, conv_weight, conv_bias, proj_weight, step_weight,
    step_bias, decay_rate, skip_gain, out_weight, carried_state,
):
    rows, feat = tokens.shape
    n_tp = lax.axis_size("tp")
    n_ctx = lax.axis_size("ctx")
    square = n_tp == 8
    shift = [(i, i + 1) for i in range(n_ctx - 1)]
    proj_wt = proj_weight.T
    decay_t = decay_rate.T
    carried_t = carried_state.T

    if square:
        p1 = flip(tokens, "tp", 1)
        px = flip(tokens, "tp", 2)
        py = flip(tokens, "tp", 4)
        pd = flip(tokens, "tp", 6)
        inner_d, = fetch([6, 7], [inner_weight], feat)
        inner, = mm([tokens, p1], [0, 1], [inner_weight], None)
        gate_acc, = mm([tokens, p1], [0, 1], [gate_weight], None)
        px = tie(px, inner, gate_acc, inner_d)
        py = tie(py, inner, gate_acc, inner_d)
        qx = flip(px, "tp", 1)
        qy = flip(py, "tp", 1)
        inner, = mm([px, qx], [2, 3], [inner_weight], [inner])
        inner, = mm([py, qy], [4, 5], [inner_weight], [inner])
        gate_acc, = mm([px, qx], [2, 3], [gate_weight], [gate_acc])
        pd = tie(pd, inner, gate_acc)
        qd = flip(pd, "tp", 1)
        inner_x, edge_x = finish(pd, qd, inner_d, inner, EDGE)
    else:
        piece = lax.all_gather(tokens, "tp", axis=1, tiled=True)
        inner_x = jnp.dot(piece, inner_weight, preferred_element_type=F32).astype(BF16)
        gate_acc = jnp.dot(piece, gate_weight, preferred_element_type=F32)
        edge_x = inner_x[rows - EDGE :]

    tail = lax.ppermute(edge_x, "ctx", shift)
    conv_x, send, keep = conv_proj(
        inner_x, tail, conv_weight, conv_bias[None, :], proj_wt, square
    )
    if square:
        part = add(keep, flip(send, "tp", 1))
        quarter = [flip(part, "tp", m) for m in (2, 4, 6)]
        cols_away = fetch_cols([7, 3, 5, 1], out_weight, feat, part)
        quarter = [tie(v, cols_away) for v in quarter]
        mine = add(part, *quarter)
        parts = (mine, flip(mine, "tp", 1))
    else:
        parts = (lax.psum(keep, "tp"),)
    end, y, cum, bc = scan(
        parts, conv_x, step_weight, step_bias[None, :], decay_t, carried_t
    )

    group, ent, bit = end, None, 1
    while bit * 2 < n_ctx:
        got = flip(group, "ctx", bit)
        if square and bit == 1:
            gate_acc, = mm([py, qy], [4, 5], [gate_weight], [tie(gate_acc, group)])
            got = tie(got, gate_acc)
        group, ent = merge(bit, decay_t, group, got, ent)
        bit *= 2
    pairs = [(i, i ^ bit) for i in range(n_ctx) if (i // bit) % 2 == 0]
    got = lax.ppermute(group, "ctx", pairs)
    if square:
        gate_acc, = mm([pd, qd], [6, 7], [gate_weight], [tie(gate_acc, group)])
        got = tie(got, gate_acc)
    gated, bound = gating(
        bit, y, cum, bc, end, got, ent, decay_t, conv_x, skip_gain[None, :], gate_acc
    )
    if square:
        away = out_held(gated, cols_away)
        got = flip(away, "tp", 1)
        near = out_blocks(gated, out_weight, [6, 2, 4, 0], feat)
        sd, sx, sy, so = add_pair(near, got)
        rd = flip(sd, "tp", 6)
        rx = flip(sx, "tp", 2)
        ry = flip(sy, "tp", 4)
        mixed = add(so, rx, ry, rd)
    else:
        partial = jnp.dot(gated, out_weight, preferred_element_type=F32).astype(BF16)
        mixed = lax.psum_scatter(partial, "tp", scatter_dimension=1, tiled=True)
    return (mixed, bound.T[None])


def solution(mesh):
    in_specs = (
        P("ctx", "tp"), P(None, "tp"), P(None, "tp"), P(None, "tp"), P("tp"), P("tp", None),
        P(None, "tp"), P("tp"), P("tp", None), P("tp"), P("tp", None), P("tp", None),
    )
    out_specs = (P("ctx", "tp"), P("ctx", "tp", None))
    return jax.shard_map(
        on_device, mesh=mesh, in_specs=in_specs, out_specs=out_specs, check_vma=False
    )
```

```python
import functools
import math

import jax
import jax.numpy as jnp
from jax import lax
from jax.experimental import pallas as pl
from jax.experimental.pallas import tpu as pltpu
from jax.sharding import PartitionSpec as P


STATE = 16
DT_RANK = 512
LANES = 128
EDGE = 8
LOG2E = math.log2(math.e)
F32 = jnp.float32
BF16 = jnp.bfloat16
VMEM = pltpu.VMEM


def flip(value, axis, mask):
    peers = lax.axis_size(axis)
    return lax.ppermute(value, axis, [(i, i ^ mask) for i in range(peers)])


def cost(flops, nbytes, trans=0):
    return pl.CostEstimate(flops=flops, bytes_accessed=nbytes, transcendentals=trans)


PIECES = 2


def params(mib):
    return pltpu.CompilerParams(vmem_limit_bytes=mib << 20)


def far(value):
    return pltpu.with_memory_space_constraint(value, pltpu.HBM)


def tie(value, *others):
    return lax.optimization_barrier((value, *others))[0]


def peer(role):
    me = lax.axis_index("tp")
    core = me % 2
    if role >= 20:
        return me ^ (4 - 2 * core) ^ (role - 20)
    if role >= 10:
        return me ^ (2 + 2 * core) ^ (role - 10)
    return me ^ role


def row_copies(masks, weights, bufs, sem, feat):
    copies = []
    piece = feat // PIECES
    for q, (w, buf) in enumerate(zip(weights, bufs)):
        for i, mask in enumerate(masks):
            for p in range(PIECES):
                at = pl.multiple_of((peer(mask)) * feat + p * piece, piece)
                copies.append(
                    pltpu.make_async_copy(
                        w.at[pl.ds(at, piece), :],
                        buf.at[pl.ds(i * feat + p * piece, piece), :],
                        sem.at[(q * len(masks) + i) * PIECES + p],
                    )
                )
    return copies


def mm_kernel(masks, n_w, has_acc, *refs):
    n_b = len(masks)
    lhs = refs[:n_b]
    w = refs[n_b : n_b + n_w]
    refs = refs[n_b + n_w :]
    acc_in = refs[:n_w] if has_acc else None
    refs = refs[n_w:] if has_acc else refs
    outs = refs[:n_w]
    bufs = refs[n_w : 2 * n_w]
    sem = refs[2 * n_w]
    feat = lhs[0].shape[1]
    piece = feat // PIECES
    copies = row_copies(masks, w, bufs, sem, feat)
    for c in copies:
        c.start()
    step = 0
    for q in range(n_w):
        total = acc_in[q][...] if has_acc else None
        for i in range(n_b):
            for p in range(PIECES):
                copies[step].wait()
                step += 1
                part = jnp.dot(
                    lhs[i][:, p * piece : (p + 1) * piece],
                    bufs[q][i * feat + p * piece : i * feat + (p + 1) * piece, :],
                    preferred_element_type=F32,
                )
                total = part if total is None else total + part
        outs[q][...] = total


def mm(blocks, masks, weights, accs):
    rows, feat = blocks[0].shape
    ch = weights[0].shape[1]
    n_w = len(weights)
    has_acc = accs is not None
    vm = pl.BlockSpec(memory_space=VMEM)
    depth = feat * len(blocks)
    return pl.pallas_call(
        functools.partial(mm_kernel, masks, n_w, has_acc),
        in_specs=[vm] * len(blocks)
        + [pl.BlockSpec(memory_space=pltpu.HBM)] * n_w
        + [vm] * (n_w if has_acc else 0),
        out_specs=[vm] * n_w,
        out_shape=[jax.ShapeDtypeStruct((rows, ch), F32)] * n_w,
        scratch_shapes=[VMEM((depth, ch), BF16)] * n_w
        + [pltpu.SemaphoreType.DMA((n_w * len(blocks) * PIECES,))],
        compiler_params=params(12),
        cost_estimate=cost(2 * rows * depth * ch * n_w, 2 * depth * ch * n_w),
    )(*blocks, *map(far, weights), *(accs or ()))


def fetch_kernel(masks, n_w, *refs):
    w = refs[:n_w]
    outs = refs[n_w + 1 : 2 * n_w + 1]
    sem = refs[2 * n_w + 1]
    copies = row_copies(masks, w, outs, sem, outs[0].shape[0] // len(masks))
    for c in copies:
        c.start()
    for c in copies:
        c.wait()


def fetch(masks, weights, feat, dep):
    ch = weights[0].shape[1]
    n_w = len(weights)
    depth = feat * len(masks)
    return pl.pallas_call(
        functools.partial(fetch_kernel, masks, n_w),
        in_specs=[pl.BlockSpec(memory_space=pltpu.HBM)] * n_w + [pl.BlockSpec(memory_space=VMEM)],
        out_specs=[pl.BlockSpec(memory_space=VMEM)] * n_w,
        out_shape=[VMEM((depth, ch), BF16)] * n_w,
        scratch_shapes=[pltpu.SemaphoreType.DMA((n_w * len(masks) * PIECES,))],
        compiler_params=params(1),
        cost_estimate=cost(0, 2 * depth * ch * n_w),
    )(*map(far, weights), dep)


def last_kernel(edge, a_ref, b_ref, w_ref, acc_ref, out_ref, edge_ref=None):
    feat = a_ref.shape[1]
    total = acc_ref[...] + jnp.dot(a_ref[...], w_ref[:feat, :], preferred_element_type=F32)
    total = total + jnp.dot(b_ref[...], w_ref[feat:, :], preferred_element_type=F32)
    out_ref[...] = total.astype(BF16)
    if edge:
        edge_ref[...] = total[total.shape[0] - edge :].astype(BF16)


def finish(a, b, w, acc, edge=0):
    rows, feat = a.shape
    ch = w.shape[1]
    vm = pl.BlockSpec(memory_space=VMEM)
    shapes = [jax.ShapeDtypeStruct((rows, ch), BF16)]
    if edge:
        shapes.append(jax.ShapeDtypeStruct((edge, ch), BF16))
    return pl.pallas_call(
        functools.partial(last_kernel, edge),
        in_specs=[vm] * 4,
        out_specs=[vm] * len(shapes),
        out_shape=shapes,
        compiler_params=params(4),
        cost_estimate=cost(4 * rows * feat * ch, 4 * feat * ch),
    )(a, b, pltpu.with_memory_space_constraint(w, VMEM), acc)


def conv_kernel(split, x_ref, tail_ref, w_ref, b_ref, pw_ref, conv_ref, send_ref, keep_ref, pad, acc):
    rows, ch = x_ref.shape
    taps = w_ref.shape[0]
    edge = tail_ref.shape[0]
    pad[0:edge, :] = tail_ref[...].astype(F32)
    pad[edge : edge + rows, :] = x_ref[...].astype(F32)
    total = jnp.broadcast_to(b_ref[...], (rows, ch))
    for k in range(taps):
        total = total + w_ref[k : k + 1, :] * pad[edge - taps + 1 + k : edge - taps + 1 + k + rows, :]
    conv = (total * jax.nn.sigmoid(total)).astype(BF16)
    conv_ref[...] = conv
    proj = lax.dot_general(conv, pw_ref[...], (((1,), (1,)), ((), ())), preferred_element_type=F32)
    if split:
        half = rows // 2
        core = lax.axis_index("tp") % 2
        acc[...] = proj
        send_ref[...] = acc[pl.ds(pl.multiple_of((1 - core) * half, half), half), :].astype(BF16)
        keep_ref[...] = acc[pl.ds(pl.multiple_of(core * half, half), half), :]
    else:
        keep_ref[...] = proj.astype(keep_ref.dtype)
        send_ref[...] = jnp.zeros(send_ref.shape, send_ref.dtype)


def conv_proj(x, tail, conv_w, conv_b, proj_wt, split):
    rows, ch = x.shape
    wide = proj_wt.shape[0]
    half = rows // 2 if split else rows
    shalf = half if split else 8
    return pl.pallas_call(
        functools.partial(conv_kernel, split),
        in_specs=[pl.BlockSpec(memory_space=VMEM)] * 5,
        out_specs=[pl.BlockSpec(memory_space=VMEM)] * 3,
        out_shape=[
            jax.ShapeDtypeStruct((rows, ch), BF16),
            jax.ShapeDtypeStruct((shalf, wide), BF16),
            jax.ShapeDtypeStruct((half, wide), F32 if split else BF16),
        ],
        scratch_shapes=[VMEM((tail.shape[0] + rows, ch), F32), VMEM((rows, wide), F32)],
        compiler_params=params(6),
        cost_estimate=cost(2 * rows * ch * wide, 2 * ch * wide),
    )(x, tail, conv_w, conv_b, proj_wt)


def spread(ref, value, groups):
    count = value.shape[0]
    for j in range(groups):
        ref[pl.ds(j, count, stride=groups), :] = value[:, j * LANES : (j + 1) * LANES]


def collect(ref, count, groups):
    return jnp.concatenate([ref[pl.ds(j, count, stride=groups), :] for j in range(groups)], axis=1)


def line(ref, at, groups):
    return jnp.broadcast_to(ref[pl.ds(at, 1), :], (groups, LANES))


def scan_kernel(
    split, *refs,
):
    n_p = 2 if split else 1
    parts = refs[:n_p]
    (conv_ref, sw_ref, sb_ref, decay_ref, carried_ref,
     end_ref, y_ref, cum_ref, c_ref,
     proj_s, step_s, drive_s, nd_s, h_s, b_ref) = refs[n_p:]
    rows, ch = conv_ref.shape
    groups = ch // LANES
    if split:
        half = rows // 2
        core = lax.axis_index("tp") % 2
        proj_s[pl.ds(pl.multiple_of(core * half, half), half), :] = parts[0][...].astype(F32)
        proj_s[pl.ds(pl.multiple_of((1 - core) * half, half), half), :] = parts[1][...].astype(F32)
    else:
        proj_s[...] = parts[0][...].astype(F32)
    for n in range(STATE):
        for ref, at in ((b_ref, DT_RANK + n), (c_ref, DT_RANK + STATE + n)):
            ref[pl.ds(n, rows, stride=STATE), :] = jnp.broadcast_to(
                proj_s[:, at : at + 1], (rows, LANES)
            )
    low = proj_s[:, :DT_RANK].astype(BF16)
    pre = jnp.dot(low, sw_ref[...], preferred_element_type=F32) + sb_ref[...]
    step = jnp.maximum(pre, 0.0) + jnp.log1p(jnp.exp(-jnp.abs(pre)))
    spread(step_s, step, groups)
    spread(drive_s, step * conv_ref[...].astype(F32), groups)
    spread(nd_s, decay_ref[...] * -LOG2E, groups)
    lead = jnp.where(lax.axis_index("ctx") == 0, 1.0, 0.0)
    spread(h_s, carried_ref[...] * lead, groups)
    nd = [nd_s[n * groups : (n + 1) * groups, :] for n in range(STATE)]
    h0 = tuple(h_s[n * groups : (n + 1) * groups, :] for n in range(STATE))

    def body(t, carry):
        h, total = carry
        at = pl.ds(pl.multiple_of(t * groups, groups), groups)
        dt = step_s[at, :]
        u = drive_s[at, :]
        total = total + dt
        cum_ref[at, :] = total
        y = None
        new = []
        for n in range(STATE):
            a = jnp.exp2(dt * nd[n])
            v = a * h[n] + u * line(b_ref, t * STATE + n, groups)
            new.append(v)
            term = v * line(c_ref, t * STATE + n, groups)
            y = term if y is None else y + term
        y_ref[at, :] = y
        return tuple(new), total

    h, total = lax.fori_loop(0, rows, body, (h0, jnp.zeros((groups, LANES), F32)), unroll=8)
    for n in range(STATE):
        h_s[n * groups : (n + 1) * groups, :] = h[n]
    end_ref[0:STATE, :] = collect(h_s, STATE, groups)
    nd_s[0:groups, :] = total
    end_ref[STATE : STATE + 1, :] = collect(nd_s, 1, groups)


def scan(parts, conv_x, step_w, step_b, decay_t, carried_t):
    rows, ch = conv_x.shape
    groups = ch // LANES
    vm = pl.BlockSpec(memory_space=VMEM)
    return pl.pallas_call(
        functools.partial(scan_kernel, len(parts) == 2),
        in_specs=[vm] * (5 + len(parts)),
        out_specs=[vm] * 4,
        out_shape=[
            jax.ShapeDtypeStruct((STATE + 1, ch), F32),
            jax.ShapeDtypeStruct((rows * groups, LANES), F32),
            jax.ShapeDtypeStruct((rows * groups, LANES), F32),
            jax.ShapeDtypeStruct((rows * STATE, LANES), F32),
        ],
        scratch_shapes=[
            VMEM((rows, parts[0].shape[1]), F32),
            VMEM((rows * groups, LANES), F32),
            VMEM((rows * groups, LANES), F32),
            VMEM((STATE * groups, LANES), F32),
            VMEM((STATE * groups, LANES), F32),
            VMEM((rows * STATE, LANES), F32),
        ],
        compiler_params=params(8),
        cost_estimate=cost(rows * ch * STATE * 8, rows * ch * 8, rows * ch * STATE),
    )(*parts, conv_x, step_w, step_b, decay_t, carried_t)


def add_kernel(*refs):
    total = refs[0][...].astype(F32)
    for r in refs[1:-1]:
        total = total + r[...].astype(F32)
    refs[-1][...] = total.astype(BF16)


def add(*values):
    vm = pl.BlockSpec(memory_space=VMEM)
    shape = values[0].shape
    size = shape[0] * shape[1]
    return pl.pallas_call(
        add_kernel,
        in_specs=[vm] * len(values),
        out_specs=vm,
        out_shape=jax.ShapeDtypeStruct(shape, BF16),
        compiler_params=params(3),
        cost_estimate=cost(size * len(values), 2 * size * len(values)),
    )(*values)


def add_pair_kernel(a_ref, b_ref, *outs):
    for i, o in enumerate(outs):
        o[...] = (a_ref[i].astype(F32) + b_ref[i].astype(F32)).astype(BF16)


def add_pair(a, b):
    vm = pl.BlockSpec(memory_space=VMEM)
    n, rows, feat = a.shape
    return pl.pallas_call(
        add_pair_kernel,
        in_specs=[vm, vm],
        out_specs=[vm] * n,
        out_shape=[jax.ShapeDtypeStruct((rows, feat), BF16)] * n,
        compiler_params=params(3),
        cost_estimate=cost(a.size, 6 * a.size),
    )(a, b)


def merge_kernel(bit, first, decay_ref, group_ref, got_ref, *refs):
    ent_ref = None if first else refs[0]
    new_ref, out_ref = refs[-2:]
    upper = (lax.axis_index("ctx") // bit) % 2 == 1
    decay = decay_ref[...]
    gh, gs = got_ref[:STATE, :], got_ref[STATE:, :]
    mh, ms = group_ref[:STATE, :], group_ref[STATE:, :]
    entering = gh if first else jnp.exp(-decay * ent_ref[STATE:, :]) * gh + ent_ref[:STATE, :]
    before = gs if first else ent_ref[STATE:, :] + gs
    keep_h = jnp.zeros_like(gh) if first else ent_ref[:STATE, :]
    keep_s = jnp.zeros_like(gs) if first else ent_ref[STATE:, :]
    out_ref[:STATE, :] = jnp.where(upper, entering, keep_h)
    out_ref[STATE:, :] = jnp.where(upper, before, keep_s)
    low = jnp.where(upper, gh, mh)
    high = jnp.where(upper, mh, gh)
    high_s = jnp.where(upper, ms, gs)
    new_ref[:STATE, :] = jnp.exp(-decay * high_s) * low + high
    new_ref[STATE:, :] = ms + gs


def merge(bit, decay_t, group, got, ent):
    vm = pl.BlockSpec(memory_space=VMEM)
    first = ent is None
    extra = () if first else (ent,)
    return pl.pallas_call(
        functools.partial(merge_kernel, bit, first),
        in_specs=[vm] * (3 + len(extra)),
        out_specs=[vm, vm],
        out_shape=[jax.ShapeDtypeStruct(group.shape, F32)] * 2,
        compiler_params=params(3),
        cost_estimate=cost(group.size * 8, group.size * 16),
    )(decay_t, group, got, *extra)


def gate_kernel(bit, first, y_ref, cum_ref, c_ref, end_ref, got_ref, decay_ref, conv_ref, skip_ref, gate_ref, *refs):
    ent_ref = None if first else refs[0]
    out_ref, bound_ref, nd_s, e_s, y_s = refs[-5:]
    rows, ch = conv_ref.shape
    groups = ch // LANES
    decay = decay_ref[...]
    upper = (lax.axis_index("ctx") // bit) % 2 == 1
    got = got_ref[:STATE, :]
    if first:
        entering = jnp.where(upper, got, jnp.zeros_like(got))
    else:
        kept = ent_ref[:STATE, :]
        entering = jnp.where(upper, jnp.exp(-decay * ent_ref[STATE:, :]) * got + kept, kept)
    bound_ref[...] = jnp.exp(-decay * end_ref[STATE:, :]) * entering + end_ref[:STATE, :]
    spread(nd_s, decay * -LOG2E, groups)
    spread(e_s, entering, groups)
    nd = [nd_s[n * groups : (n + 1) * groups, :] for n in range(STATE)]
    ent = [e_s[n * groups : (n + 1) * groups, :] for n in range(STATE)]

    def body(t, carry):
        at = pl.ds(pl.multiple_of(t * groups, groups), groups)
        total = cum_ref[at, :]
        y = y_ref[at, :]
        for n in range(STATE):
            y = y + jnp.exp2(total * nd[n]) * ent[n] * line(c_ref, t * STATE + n, groups)
        y_s[at, :] = y
        return carry

    lax.fori_loop(0, rows, body, 0, unroll=8)
    y = collect(y_s, rows, groups)
    gate = gate_ref[...].astype(BF16).astype(F32)
    out = (y + skip_ref[...] * conv_ref[...].astype(F32)) * (gate * jax.nn.sigmoid(gate))
    out_ref[...] = out.astype(BF16)


def gating(bit, y, cum, bc, end, got, ent, decay_t, conv_x, skip, gate):
    rows, ch = conv_x.shape
    groups = ch // LANES
    vm = pl.BlockSpec(memory_space=VMEM)
    first = ent is None
    extra = () if first else (ent,)
    return pl.pallas_call(
        functools.partial(gate_kernel, bit, first),
        in_specs=[vm] * (9 + len(extra)),
        out_specs=[vm, vm],
        out_shape=[
            jax.ShapeDtypeStruct((rows, ch), BF16),
            jax.ShapeDtypeStruct((STATE, ch), F32),
        ],
        scratch_shapes=[
            VMEM((STATE * groups, LANES), F32),
            VMEM((STATE * groups, LANES), F32),
            VMEM((rows * groups, LANES), F32),
        ],
        compiler_params=params(8),
        cost_estimate=cost(rows * ch * STATE * 6, rows * ch * 8, rows * ch * STATE),
    )(y, cum, bc, end, got, decay_t, conv_x, skip, gate, *extra)


def col_copies(masks, w, buf, sem, feat):
    copies = []
    for i, mask in enumerate(masks):
        at = pl.multiple_of((peer(mask)) * feat, feat)
        copies.append(
            pltpu.make_async_copy(w.at[:, pl.ds(at, feat)], buf.at[i], sem.at[i])
        )
    return copies


def cols_kernel(masks, w_ref, dep_ref, out_ref, sem):
    copies = col_copies(masks, w_ref, out_ref, sem, out_ref.shape[2])
    for c in copies:
        c.start()
    for c in copies:
        c.wait()


def fetch_cols(masks, weight, feat, dep):
    ch = weight.shape[0]
    return pl.pallas_call(
        functools.partial(cols_kernel, masks),
        in_specs=[
            pl.BlockSpec(memory_space=pltpu.HBM),
            pl.BlockSpec(memory_space=VMEM),
        ],
        out_specs=pl.BlockSpec(memory_space=VMEM),
        out_shape=VMEM((len(masks), ch, feat), BF16),
        scratch_shapes=[pltpu.SemaphoreType.DMA((len(masks),))],
        compiler_params=params(1),
        cost_estimate=cost(0, 2 * ch * feat * len(masks)),
    )(far(weight), dep)


def out_held_kernel(g_ref, w_ref, o_ref):
    for i in range(w_ref.shape[0]):
        o_ref[i] = jnp.dot(g_ref[...], w_ref[i], preferred_element_type=F32).astype(o_ref.dtype)


def out_held(gated, cols):
    rows, ch = gated.shape
    n, _, feat = cols.shape
    vm = pl.BlockSpec(memory_space=VMEM)
    return pl.pallas_call(
        out_held_kernel,
        in_specs=[vm, vm],
        out_specs=vm,
        out_shape=jax.ShapeDtypeStruct((n, rows, feat), BF16),
        compiler_params=params(4),
        cost_estimate=cost(2 * rows * ch * feat * n, 2 * ch * feat * n),
    )(gated, pltpu.with_memory_space_constraint(cols, VMEM))


def out_kernel(masks, g_ref, w_ref, o_ref, buf, sem):
    copies = col_copies(masks, w_ref, buf, sem, o_ref.shape[2])
    for c in copies:
        c.start()
    for i, c in enumerate(copies):
        c.wait()
        o_ref[i] = jnp.dot(g_ref[...], buf[i], preferred_element_type=F32).astype(o_ref.dtype)


def out_blocks(gated, weight, masks, feat):
    rows, ch = gated.shape
    n = len(masks)
    vm = pl.BlockSpec(memory_space=VMEM)
    return pl.pallas_call(
        functools.partial(out_kernel, masks),
        in_specs=[vm, pl.BlockSpec(memory_space=pltpu.HBM)],
        out_specs=vm,
        out_shape=jax.ShapeDtypeStruct((n, rows, feat), BF16),
        scratch_shapes=[VMEM((n, ch, feat), BF16), pltpu.SemaphoreType.DMA((n,))],
        compiler_params=params(12),
        cost_estimate=cost(2 * rows * ch * feat * n, 2 * ch * feat * n),
    )(gated, far(weight))


def on_device(
    tokens, inner_weight, gate_weight, conv_weight, conv_bias, proj_weight, step_weight,
    step_bias, decay_rate, skip_gain, out_weight, carried_state,
):
    rows, feat = tokens.shape
    n_tp = lax.axis_size("tp")
    n_ctx = lax.axis_size("ctx")
    square = n_tp == 8
    shift = [(i, i + 1) for i in range(n_ctx - 1)]
    proj_wt = proj_weight.T
    decay_t = decay_rate.T
    carried_t = carried_state.T

    if square:
        p1 = flip(tokens, "tp", 1)
        px = flip(tokens, "tp", 2)
        py = flip(tokens, "tp", 4)
        pd = flip(tokens, "tp", 6)
        inner, gate_acc = mm([tokens, p1], [0, 1], [inner_weight, gate_weight], None)
        px = tie(px, inner)
        py = tie(py, inner)
        qx = flip(px, "tp", 1)
        qy = flip(py, "tp", 1)
        inner, = mm([px, qx, py, qy], [2, 3, 4, 5], [inner_weight], [inner])
        pd = tie(pd, inner)
        qd = flip(pd, "tp", 1)
        inner_d, = fetch([6, 7], [inner_weight], feat, pd)
        qd = tie(qd, inner_d)
        inner_x, edge_x = finish(pd, qd, inner_d, inner, EDGE)
    else:
        piece = lax.all_gather(tokens, "tp", axis=1, tiled=True)
        inner_x = jnp.dot(piece, inner_weight, preferred_element_type=F32).astype(BF16)
        gate_acc = jnp.dot(piece, gate_weight, preferred_element_type=F32)
        edge_x = inner_x[rows - EDGE :]

    tail = lax.ppermute(edge_x, "ctx", shift)
    if square:
        gate_acc, = mm([px], [2], [gate_weight], [tie(gate_acc, edge_x)])
        tail = tie(tail, gate_acc)
    conv_x, send, keep = conv_proj(
        inner_x, tail, conv_weight, conv_bias[None, :], proj_wt, square
    )
    if square:
        part = add(keep, flip(send, "tp", 1))
        quarter = [flip(part, "tp", m) for m in (2, 4, 6)]
        cols_away = fetch_cols([7, 21, 11, 1], out_weight, feat, part)
        quarter = [tie(v, cols_away) for v in quarter]
        mine = add(part, *quarter)
        parts = (mine, flip(mine, "tp", 1))
    else:
        parts = (lax.psum(keep, "tp"),)
    end, y, cum, bc = scan(
        parts, conv_x, step_weight, step_bias[None, :], decay_t, carried_t
    )

    group, ent, bit = end, None, 1
    while bit * 2 < n_ctx:
        got = flip(group, "ctx", bit)
        if square and bit == 1:
            gate_acc, = mm([qx, py, qy], [3, 4, 5], [gate_weight], [tie(gate_acc, group)])
            got = tie(got, gate_acc)
        group, ent = merge(bit, decay_t, group, got, ent)
        bit *= 2
    pairs = [(i, i ^ bit) for i in range(n_ctx) if (i // bit) % 2 == 0]
    got = lax.ppermute(group, "ctx", pairs)
    if square:
        gate_acc, = mm([pd, qd], [6, 7], [gate_weight], [tie(gate_acc, group)])
        got = tie(got, gate_acc)
    gated, bound = gating(
        bit, y, cum, bc, end, got, ent, decay_t, conv_x, skip_gain[None, :], gate_acc
    )
    if square:
        away = out_held(gated, cols_away)
        got = flip(away, "tp", 1)
        near = out_blocks(gated, out_weight, [6, 10, 20, 0], feat)
        sd, sf, ss, so = add_pair(near, got)
        to_first = [(i, i ^ (2 + 2 * (i % 2))) for i in range(n_tp)]
        to_second = [(i, i ^ (4 - 2 * (i % 2))) for i in range(n_tp)]
        rd = lax.ppermute(sd, "tp", to_first)
        rf = lax.ppermute(sf, "tp", to_first)
        rs = lax.ppermute(add(ss, rd), "tp", to_second)
        mixed = add(so, rf, rs)
    else:
        partial = jnp.dot(gated, out_weight, preferred_element_type=F32).astype(BF16)
        mixed = lax.psum_scatter(partial, "tp", scatter_dimension=1, tiled=True)
    return (mixed, bound.T[None])


def solution(mesh):
    in_specs = (
        P("ctx", "tp"), P(None, "tp"), P(None, "tp"), P(None, "tp"), P("tp"), P("tp", None),
        P(None, "tp"), P("tp"), P("tp", None), P("tp"), P("tp", None), P("tp", None),
    )
    out_specs = (P("ctx", "tp"), P("ctx", "tp", None))
    return jax.shard_map(
        on_device, mesh=mesh, in_specs=in_specs, out_specs=out_specs, check_vma=False
    )
```

```python
import functools
import math

import jax
import jax.numpy as jnp
from jax import lax
from jax.experimental import pallas as pl
from jax.experimental.pallas import tpu as pltpu
from jax.sharding import PartitionSpec as P


STATE = 16
DT_RANK = 512
LANES = 128
EDGE = 8
LOG2E = math.log2(math.e)
F32 = jnp.float32
BF16 = jnp.bfloat16
VMEM = pltpu.VMEM


def flip(value, axis, mask):
    peers = lax.axis_size(axis)
    return lax.ppermute(value, axis, [(i, i ^ mask) for i in range(peers)])


def cost(flops, nbytes, trans=0):
    return pl.CostEstimate(flops=flops, bytes_accessed=nbytes, transcendentals=trans)


PIECES = 2


def params(mib):
    return pltpu.CompilerParams(vmem_limit_bytes=mib << 20)


def far(value):
    return pltpu.with_memory_space_constraint(value, pltpu.HBM)


def tie(value, *others):
    return lax.optimization_barrier((value, *others))[0]


def peer(role):
    me = lax.axis_index("tp")
    core = me % 2
    if role >= 20:
        return me ^ (4 - 2 * core) ^ (role - 20)
    if role >= 10:
        return me ^ (2 + 2 * core) ^ (role - 10)
    return me ^ role


def row_copies(masks, weights, bufs, sem, feat):
    copies = []
    piece = feat // PIECES
    for q, (w, buf) in enumerate(zip(weights, bufs)):
        for i, mask in enumerate(masks):
            for p in range(PIECES):
                at = pl.multiple_of((peer(mask)) * feat + p * piece, piece)
                copies.append(
                    pltpu.make_async_copy(
                        w.at[pl.ds(at, piece), :],
                        buf.at[pl.ds(i * feat + p * piece, piece), :],
                        sem.at[(q * len(masks) + i) * PIECES + p],
                    )
                )
    return copies


def stream_kernel(masks, n_w, has_acc, *refs):
    n_b = len(masks)
    lhs = refs[:n_b]
    w = refs[n_b : n_b + n_w]
    refs = refs[n_b + n_w :]
    acc_in = refs[:n_w] if has_acc else None
    refs = refs[n_w:] if has_acc else refs
    outs = refs[:n_w]
    bufs = refs[n_w : 2 * n_w]
    sem = refs[2 * n_w]
    feat = lhs[0].shape[1]
    piece = feat // PIECES
    copies = row_copies(masks, w, bufs, sem, feat)
    own, own_sem = refs[2 * n_w + 1 :]
    load = pltpu.make_async_copy(lhs[-1], own, own_sem)
    load.start()
    for c in copies:
        c.start()
    lhs = tuple(lhs[:-1]) + (own,)
    step = 0
    for q in range(n_w):
        total = acc_in[q][...] if has_acc else None
        for i in range(n_b):
            if i == n_b - 1 and q == 0:
                load.wait()
            for p in range(PIECES):
                copies[step].wait()
                step += 1
                part = jnp.dot(
                    lhs[i][:, p * piece : (p + 1) * piece],
                    bufs[q][i * feat + p * piece : i * feat + (p + 1) * piece, :],
                    preferred_element_type=F32,
                )
                total = part if total is None else total + part
        outs[q][...] = total


def stream_mm(blocks, masks, weights, accs):
    rows, feat = blocks[0].shape
    ch = weights[0].shape[1]
    n_w = len(weights)
    has_acc = accs is not None
    vm = pl.BlockSpec(memory_space=VMEM)
    depth = feat * len(blocks)
    return pl.pallas_call(
        functools.partial(stream_kernel, masks, n_w, has_acc),
        in_specs=[vm] * (len(blocks) - 1)
        + [pl.BlockSpec(memory_space=pltpu.HBM)]
        + [pl.BlockSpec(memory_space=pltpu.HBM)] * n_w
        + [vm] * (n_w if has_acc else 0),
        out_specs=[vm] * n_w,
        out_shape=[jax.ShapeDtypeStruct((rows, ch), F32)] * n_w,
        scratch_shapes=[VMEM((depth, ch), BF16)] * n_w
        + [pltpu.SemaphoreType.DMA((n_w * len(blocks) * PIECES,))]
        + [VMEM((rows, feat), BF16), pltpu.SemaphoreType.DMA],
        compiler_params=params(12),
        cost_estimate=cost(2 * rows * depth * ch * n_w, 2 * depth * ch * n_w),
    )(*blocks[:-1], far(blocks[-1]), *map(far, weights), *(accs or ()))


def held(value):
    return pltpu.with_memory_space_constraint(value, VMEM)


def mm_kernel(roles, has_acc, edge, *refs):
    n_b = len(roles)
    lhs = refs[:n_b]
    w_ref = refs[n_b]
    total = refs[n_b + 1][...] if has_acc else None
    outs = refs[n_b + 1 + has_acc :]
    feat = lhs[0].shape[1]
    for x, role in zip(lhs, roles):
        at = pl.ds(pl.multiple_of(peer(role) * feat, feat), feat)
        part = jnp.dot(x[...], w_ref[at, :], preferred_element_type=F32)
        total = part if total is None else total + part
    outs[0][...] = total.astype(outs[0].dtype)
    if edge:
        outs[1][...] = total[total.shape[0] - edge :].astype(BF16)


def mm(blocks, roles, weight, acc, edge=0):
    rows, feat = blocks[0].shape
    ch = weight.shape[1]
    vm = pl.BlockSpec(memory_space=VMEM)
    shapes = [jax.ShapeDtypeStruct((rows, ch), BF16 if edge else F32)]
    if edge:
        shapes.append(jax.ShapeDtypeStruct((edge, ch), BF16))
    extra = () if acc is None else (acc,)
    n = len(blocks)
    return pl.pallas_call(
        functools.partial(mm_kernel, roles, len(extra), edge),
        in_specs=[vm] * (n + 1 + len(extra)),
        out_specs=[vm] * len(shapes),
        out_shape=shapes,
        compiler_params=params(5 if n > 5 else 4),
        cost_estimate=cost(2 * n * rows * feat * ch, 2 * n * feat * ch),
    )(*blocks, weight, *extra)


def conv_kernel(split, x_ref, tail_ref, w_ref, b_ref, pw_ref, conv_ref, send_ref, keep_ref, pad, acc):
    rows, ch = x_ref.shape
    taps = w_ref.shape[0]
    edge = tail_ref.shape[0]
    pad[0:edge, :] = tail_ref[...].astype(F32)
    pad[edge : edge + rows, :] = x_ref[...].astype(F32)
    total = jnp.broadcast_to(b_ref[...], (rows, ch))
    for k in range(taps):
        total = total + w_ref[k : k + 1, :] * pad[edge - taps + 1 + k : edge - taps + 1 + k + rows, :]
    conv = (total * jax.nn.sigmoid(total)).astype(BF16)
    conv_ref[...] = conv
    proj = lax.dot_general(conv, pw_ref[...], (((1,), (1,)), ((), ())), preferred_element_type=F32)
    if split:
        half = rows // 2
        core = lax.axis_index("tp") % 2
        acc[...] = proj
        send_ref[...] = acc[pl.ds(pl.multiple_of((1 - core) * half, half), half), :].astype(BF16)
        keep_ref[...] = acc[pl.ds(pl.multiple_of(core * half, half), half), :]
    else:
        keep_ref[...] = proj.astype(keep_ref.dtype)
        send_ref[...] = jnp.zeros(send_ref.shape, send_ref.dtype)


def conv_proj(x, tail, conv_w, conv_b, proj_wt, split):
    rows, ch = x.shape
    wide = proj_wt.shape[0]
    half = rows // 2 if split else rows
    shalf = half if split else 8
    return pl.pallas_call(
        functools.partial(conv_kernel, split),
        in_specs=[pl.BlockSpec(memory_space=VMEM)] * 5,
        out_specs=[pl.BlockSpec(memory_space=VMEM)] * 3,
        out_shape=[
            jax.ShapeDtypeStruct((rows, ch), BF16),
            jax.ShapeDtypeStruct((shalf, wide), BF16),
            jax.ShapeDtypeStruct((half, wide), F32 if split else BF16),
        ],
        scratch_shapes=[VMEM((tail.shape[0] + rows, ch), F32), VMEM((rows, wide), F32)],
        compiler_params=params(6),
        cost_estimate=cost(2 * rows * ch * wide, 2 * ch * wide),
    )(x, tail, conv_w, conv_b, proj_wt)


def spread(ref, value, groups):
    count = value.shape[0]
    for j in range(groups):
        ref[pl.ds(j, count, stride=groups), :] = value[:, j * LANES : (j + 1) * LANES]


def collect(ref, count, groups):
    return jnp.concatenate([ref[pl.ds(j, count, stride=groups), :] for j in range(groups)], axis=1)


def line(ref, at, groups):
    return jnp.broadcast_to(ref[pl.ds(at, 1), :], (groups, LANES))


def scan_kernel(
    split, *refs,
):
    n_p = 2 if split else 1
    parts = refs[:n_p]
    (conv_ref, sw_ref, sb_ref, decay_ref, carried_ref,
     end_ref, pack_ref, y_ref, cum_ref, c_ref,
     proj_s, step_s, drive_s, nd_s, h_s, b_ref) = refs[n_p:]
    rows, ch = conv_ref.shape
    groups = ch // LANES
    if split:
        half = rows // 2
        core = lax.axis_index("tp") % 2
        proj_s[pl.ds(pl.multiple_of(core * half, half), half), :] = parts[0][...].astype(F32)
        proj_s[pl.ds(pl.multiple_of((1 - core) * half, half), half), :] = parts[1][...].astype(F32)
    else:
        proj_s[...] = parts[0][...].astype(F32)
    for n in range(STATE):
        for ref, at in ((b_ref, DT_RANK + n), (c_ref, DT_RANK + STATE + n)):
            ref[pl.ds(n, rows, stride=STATE), :] = jnp.broadcast_to(
                proj_s[:, at : at + 1], (rows, LANES)
            )
    low = proj_s[:, :DT_RANK].astype(BF16)
    pre = jnp.dot(low, sw_ref[...], preferred_element_type=F32) + sb_ref[...]
    step = jnp.maximum(pre, 0.0) + jnp.log1p(jnp.exp(-jnp.abs(pre)))
    spread(step_s, step, groups)
    spread(drive_s, step * conv_ref[...].astype(F32), groups)
    spread(nd_s, decay_ref[...] * -LOG2E, groups)
    lead = jnp.where(lax.axis_index("ctx") == 0, 1.0, 0.0)
    spread(h_s, carried_ref[...] * lead, groups)
    nd = [nd_s[n * groups : (n + 1) * groups, :] for n in range(STATE)]
    h0 = tuple(h_s[n * groups : (n + 1) * groups, :] for n in range(STATE))

    def body(t, carry):
        h, total = carry
        at = pl.ds(pl.multiple_of(t * groups, groups), groups)
        dt = step_s[at, :]
        u = drive_s[at, :]
        total = total + dt
        cum_ref[at, :] = total
        y = None
        new = []
        for n in range(STATE):
            a = jnp.exp2(dt * nd[n])
            v = a * h[n] + u * line(b_ref, t * STATE + n, groups)
            new.append(v)
            term = v * line(c_ref, t * STATE + n, groups)
            y = term if y is None else y + term
        y_ref[at, :] = y
        return tuple(new), total

    h, total = lax.fori_loop(0, rows, body, (h0, jnp.zeros((groups, LANES), F32)), unroll=8)
    for n in range(STATE):
        h_s[n * groups : (n + 1) * groups, :] = h[n]
    end_ref[0:STATE, :] = collect(h_s, STATE, groups)
    nd_s[0:groups, :] = total
    end_ref[STATE : STATE + 1, :] = collect(nd_s, 1, groups)
    pack_ref[...] = end_ref[...].astype(BF16)


def scan(parts, conv_x, step_w, step_b, decay_t, carried_t):
    rows, ch = conv_x.shape
    groups = ch // LANES
    vm = pl.BlockSpec(memory_space=VMEM)
    return pl.pallas_call(
        functools.partial(scan_kernel, len(parts) == 2),
        in_specs=[vm] * (5 + len(parts)),
        out_specs=[vm] * 5,
        out_shape=[
            jax.ShapeDtypeStruct((STATE + 1, ch), F32),
            jax.ShapeDtypeStruct((STATE + 1, ch), BF16),
            jax.ShapeDtypeStruct((rows * groups, LANES), F32),
            jax.ShapeDtypeStruct((rows * groups, LANES), F32),
            jax.ShapeDtypeStruct((rows * STATE, LANES), F32),
        ],
        scratch_shapes=[
            VMEM((rows, parts[0].shape[1]), F32),
            VMEM((rows * groups, LANES), F32),
            VMEM((rows * groups, LANES), F32),
            VMEM((STATE * groups, LANES), F32),
            VMEM((STATE * groups, LANES), F32),
            VMEM((rows * STATE, LANES), F32),
        ],
        compiler_params=params(8),
        cost_estimate=cost(rows * ch * STATE * 8, rows * ch * 8, rows * ch * STATE),
    )(*parts, conv_x, step_w, step_b, decay_t, carried_t)


def add_kernel(*refs):
    total = refs[0][...].astype(F32)
    for r in refs[1:-1]:
        total = total + r[...].astype(F32)
    refs[-1][...] = total.astype(BF16)


def add(*values):
    vm = pl.BlockSpec(memory_space=VMEM)
    shape = values[0].shape
    size = shape[0] * shape[1]
    return pl.pallas_call(
        add_kernel,
        in_specs=[vm] * len(values),
        out_specs=vm,
        out_shape=jax.ShapeDtypeStruct(shape, BF16),
        compiler_params=params(3),
        cost_estimate=cost(size * len(values), 2 * size * len(values)),
    )(*values)


def add_pair_kernel(a_ref, b_ref, *outs):
    for i, o in enumerate(outs):
        o[...] = (a_ref[i].astype(F32) + b_ref[i].astype(F32)).astype(BF16)


def add_pair(a, b):
    vm = pl.BlockSpec(memory_space=VMEM)
    n, rows, feat = a.shape
    return pl.pallas_call(
        add_pair_kernel,
        in_specs=[vm, vm],
        out_specs=[vm] * n,
        out_shape=[jax.ShapeDtypeStruct((rows, feat), BF16)] * n,
        compiler_params=params(3),
        cost_estimate=cost(a.size, 6 * a.size),
    )(a, b)


def merge_kernel(bit, first, decay_ref, group_ref, got_ref, *refs):
    ent_ref = None if first else refs[0]
    new_ref, pack_ref, out_ref = refs[-3:]
    upper = (lax.axis_index("ctx") // bit) % 2 == 1
    decay = decay_ref[...]
    got = got_ref[...].astype(F32)
    gh, gs = got[:STATE], got[STATE:]
    mh, ms = group_ref[:STATE, :], group_ref[STATE:, :]
    entering = gh if first else jnp.exp(-decay * ent_ref[STATE:, :]) * gh + ent_ref[:STATE, :]
    before = gs if first else ent_ref[STATE:, :] + gs
    keep_h = jnp.zeros_like(gh) if first else ent_ref[:STATE, :]
    keep_s = jnp.zeros_like(gs) if first else ent_ref[STATE:, :]
    out_ref[:STATE, :] = jnp.where(upper, entering, keep_h)
    out_ref[STATE:, :] = jnp.where(upper, before, keep_s)
    low = jnp.where(upper, gh, mh)
    high = jnp.where(upper, mh, gh)
    high_s = jnp.where(upper, ms, gs)
    new_ref[:STATE, :] = jnp.exp(-decay * high_s) * low + high
    new_ref[STATE:, :] = ms + gs
    pack_ref[...] = new_ref[...].astype(BF16)


def merge(bit, decay_t, group, got, ent):
    vm = pl.BlockSpec(memory_space=VMEM)
    first = ent is None
    extra = () if first else (ent,)
    return pl.pallas_call(
        functools.partial(merge_kernel, bit, first),
        in_specs=[vm] * (3 + len(extra)),
        out_specs=[vm] * 3,
        out_shape=[
            jax.ShapeDtypeStruct(group.shape, F32),
            jax.ShapeDtypeStruct(group.shape, BF16),
            jax.ShapeDtypeStruct(group.shape, F32),
        ],
        compiler_params=params(3),
        cost_estimate=cost(group.size * 8, group.size * 16),
    )(decay_t, group, got, *extra)


def gate_kernel(bit, first, y_ref, cum_ref, c_ref, end_ref, got_ref, decay_ref, conv_ref, skip_ref, gate_ref, *refs):
    ent_ref = None if first else refs[0]
    out_ref, bound_ref, nd_s, e_s, y_s = refs[-5:]
    rows, ch = conv_ref.shape
    groups = ch // LANES
    decay = decay_ref[...]
    upper = (lax.axis_index("ctx") // bit) % 2 == 1
    got = got_ref[...].astype(F32)[:STATE]
    if first:
        entering = jnp.where(upper, got, jnp.zeros_like(got))
    else:
        kept = ent_ref[:STATE, :]
        entering = jnp.where(upper, jnp.exp(-decay * ent_ref[STATE:, :]) * got + kept, kept)
    bound_ref[...] = jnp.exp(-decay * end_ref[STATE:, :]) * entering + end_ref[:STATE, :]
    spread(nd_s, decay * -LOG2E, groups)
    spread(e_s, entering, groups)
    nd = [nd_s[n * groups : (n + 1) * groups, :] for n in range(STATE)]
    ent = [e_s[n * groups : (n + 1) * groups, :] for n in range(STATE)]

    def body(t, carry):
        at = pl.ds(pl.multiple_of(t * groups, groups), groups)
        total = cum_ref[at, :]
        y = y_ref[at, :]
        for n in range(STATE):
            y = y + jnp.exp2(total * nd[n]) * ent[n] * line(c_ref, t * STATE + n, groups)
        y_s[at, :] = y
        return carry

    lax.fori_loop(0, rows, body, 0, unroll=8)
    y = collect(y_s, rows, groups)
    gate = gate_ref[...].astype(BF16).astype(F32)
    out = (y + skip_ref[...] * conv_ref[...].astype(F32)) * (gate * jax.nn.sigmoid(gate))
    out_ref[...] = out.astype(BF16)


def gating(bit, y, cum, bc, end, got, ent, decay_t, conv_x, skip, gate):
    rows, ch = conv_x.shape
    groups = ch // LANES
    vm = pl.BlockSpec(memory_space=VMEM)
    first = ent is None
    extra = () if first else (ent,)
    return pl.pallas_call(
        functools.partial(gate_kernel, bit, first),
        in_specs=[vm] * (9 + len(extra)),
        out_specs=[vm, vm],
        out_shape=[
            jax.ShapeDtypeStruct((rows, ch), BF16),
            jax.ShapeDtypeStruct((STATE, ch), F32),
        ],
        scratch_shapes=[
            VMEM((STATE * groups, LANES), F32),
            VMEM((STATE * groups, LANES), F32),
            VMEM((rows * groups, LANES), F32),
        ],
        compiler_params=params(8),
        cost_estimate=cost(rows * ch * STATE * 6, rows * ch * 8, rows * ch * STATE),
    )(y, cum, bc, end, got, decay_t, conv_x, skip, gate, *extra)


def out_stack_kernel(masks, g_ref, w_ref, out):
    feat = out.shape[2]
    for i, mask in enumerate(masks):
        at = pl.ds(pl.multiple_of(peer(mask) * feat, feat), feat)
        out[i] = jnp.dot(g_ref[...], w_ref[:, at], preferred_element_type=F32).astype(BF16)


def out_blocks(gated, weight, masks, feat):
    rows, ch = gated.shape
    n = len(masks)
    vm = pl.BlockSpec(memory_space=VMEM)
    return pl.pallas_call(
        functools.partial(out_stack_kernel, masks),
        in_specs=[vm, vm],
        out_specs=vm,
        out_shape=jax.ShapeDtypeStruct((n, rows, feat), BF16),
        compiler_params=params(4),
        cost_estimate=cost(2 * rows * ch * feat * n, 2 * ch * feat * n),
    )(gated, weight)


def on_device(
    tokens, inner_weight, gate_weight, conv_weight, conv_bias, proj_weight, step_weight,
    step_bias, decay_rate, skip_gain, out_weight, carried_state,
):
    rows, feat = tokens.shape
    n_tp = lax.axis_size("tp")
    n_ctx = lax.axis_size("ctx")
    square = n_tp == 8
    shift = [(i, i + 1) for i in range(n_ctx - 1)]
    proj_wt = proj_weight.T
    decay_t = decay_rate.T
    carried_t = carried_state.T

    if square:
        to_first = [(i, i ^ (2 + 2 * (i % 2))) for i in range(n_tp)]
        to_second = [(i, i ^ (4 - 2 * (i % 2))) for i in range(n_tp)]
        p1 = flip(tokens, "tp", 1)
        vs = lax.ppermute(tokens, "tp", to_second)
        inner, = stream_mm([tokens], [0], [inner_weight], None)
        vf = lax.ppermute(tie(tokens, inner), "tp", to_first)
        vs = tie(vs, inner)
        vd = lax.ppermute(vs, "tp", to_first)
        qs = flip(vs, "tp", 1)
        qf = flip(vf, "tp", 1)
        inner_w, gate_w = held(inner_weight), held(gate_weight)
        inner, = mm([p1, vs, qs, vf, qf], [1, 20, 11, 10, 21], inner_w, inner)
        vd = tie(vd, inner)
        qd = flip(vd, "tp", 1)
        inner_x, edge_x = mm([vd, qd], [6, 7], inner_w, inner, EDGE)
    else:
        piece = lax.all_gather(tokens, "tp", axis=1, tiled=True)
        inner_x = jnp.dot(piece, inner_weight, preferred_element_type=F32).astype(BF16)
        gate_acc = jnp.dot(piece, gate_weight, preferred_element_type=F32)
        edge_x = inner_x[rows - EDGE :]

    tail = lax.ppermute(edge_x, "ctx", shift)
    conv_x, send, keep = conv_proj(
        inner_x, tail, conv_weight, conv_bias[None, :], proj_wt, square
    )
    if square:
        part = add(keep, flip(send, "tp", 1))
        quarter = [flip(part, "tp", m) for m in (2, 4, 6)]
        blocks = [tokens, p1, vs, qs, vf, qf, vd, qd]
        gate_acc, = mm(
            [tie(tokens, part), *blocks[1:]], [0, 1, 20, 11, 10, 21, 6, 7], gate_w, None
        )
        quarter = [tie(v, gate_acc) for v in quarter]
        mine = add(part, *quarter)
        parts = (mine, flip(mine, "tp", 1))
    else:
        parts = (lax.psum(keep, "tp"),)
    end, packet, y, cum, bc = scan(
        parts, conv_x, step_weight, step_bias[None, :], decay_t, carried_t
    )

    group, ent, bit = end, None, 1
    while bit * 2 < n_ctx:
        got = flip(packet, "ctx", bit)
        group, packet, ent = merge(bit, decay_t, group, got, ent)
        bit *= 2
    pairs = [(i, i ^ bit) for i in range(n_ctx) if (i // bit) % 2 == 0]
    got = lax.ppermute(packet, "ctx", pairs)
    gated, bound = gating(
        bit, y, cum, bc, end, got, ent, decay_t, conv_x, skip_gain[None, :], gate_acc
    )
    if square:
        out_weight = pltpu.with_memory_space_constraint(out_weight, VMEM)
        away = out_blocks(gated, out_weight, [7, 21], feat)
        got = flip(away, "tp", 1)
        away_b = out_blocks(gated, out_weight, [11, 1], feat)
        got_b = flip(away_b, "tp", 1)
        near = out_blocks(gated, out_weight, [6, 10], feat)
        sd, sf = add_pair(near, tie(got, away_b))
        near_b = out_blocks(gated, out_weight, [20, 0], feat)
        ss, so = add_pair(near_b, got_b)
        rd = lax.ppermute(sd, "tp", to_first)
        rf = lax.ppermute(sf, "tp", to_first)
        rs = lax.ppermute(add(ss, rd), "tp", to_second)
        mixed = add(so, rf, rs)
    else:
        partial = jnp.dot(gated, out_weight, preferred_element_type=F32).astype(BF16)
        mixed = lax.psum_scatter(partial, "tp", scatter_dimension=1, tiled=True)
    return (mixed, bound.T[None])


def solution(mesh):
    in_specs = (
        P("ctx", "tp"), P(None, "tp"), P(None, "tp"), P(None, "tp"), P("tp"), P("tp", None),
        P(None, "tp"), P("tp"), P("tp", None), P("tp"), P("tp", None), P("tp", None),
    )
    out_specs = (P("ctx", "tp"), P("ctx", "tp", None))
    return jax.shard_map(
        on_device, mesh=mesh, in_specs=in_specs, out_specs=out_specs, check_vma=False
    )
```

```python
import functools
import math

import jax
import jax.numpy as jnp
from jax import lax
from jax.experimental import pallas as pl
from jax.experimental.pallas import tpu as pltpu
from jax.sharding import PartitionSpec as P


STATE = 16
DT_RANK = 512
LANES = 128
EDGE = 8
LOG2E = math.log2(math.e)
F32 = jnp.float32
BF16 = jnp.bfloat16
VMEM = pltpu.VMEM


def flip(value, axis, mask):
    peers = lax.axis_size(axis)
    return lax.ppermute(value, axis, [(i, i ^ mask) for i in range(peers)])


def cost(flops, nbytes, trans=0):
    return pl.CostEstimate(flops=flops, bytes_accessed=nbytes, transcendentals=trans)


PIECES = 2


def params(mib):
    return pltpu.CompilerParams(vmem_limit_bytes=mib << 20)


def far(value):
    return pltpu.with_memory_space_constraint(value, pltpu.HBM)


def tie(value, *others):
    return lax.optimization_barrier((value, *others))[0]


def peer(role):
    me = lax.axis_index("tp")
    core = me % 2
    if role >= 20:
        return me ^ (4 - 2 * core) ^ (role - 20)
    if role >= 10:
        return me ^ (2 + 2 * core) ^ (role - 10)
    return me ^ role


def row_copies(masks, weights, bufs, sem, feat):
    copies = []
    piece = feat // PIECES
    for q, (w, buf) in enumerate(zip(weights, bufs)):
        for i, mask in enumerate(masks):
            for p in range(PIECES):
                at = pl.multiple_of((peer(mask)) * feat + p * piece, piece)
                copies.append(
                    pltpu.make_async_copy(
                        w.at[pl.ds(at, piece), :],
                        buf.at[pl.ds(i * feat + p * piece, piece), :],
                        sem.at[(q * len(masks) + i) * PIECES + p],
                    )
                )
    return copies


def stream_kernel(masks, n_w, has_acc, *refs):
    n_b = len(masks)
    lhs = refs[:n_b]
    w = refs[n_b : n_b + n_w]
    refs = refs[n_b + n_w :]
    acc_in = refs[:n_w] if has_acc else None
    refs = refs[n_w:] if has_acc else refs
    outs = refs[:n_w]
    bufs = refs[n_w : 2 * n_w]
    sem = refs[2 * n_w]
    feat = lhs[0].shape[1]
    piece = feat // PIECES
    copies = row_copies(masks, w, bufs, sem, feat)
    own, own_sem = refs[2 * n_w + 1 :]
    load = pltpu.make_async_copy(lhs[-1], own, own_sem)
    load.start()
    for c in copies:
        c.start()
    lhs = tuple(lhs[:-1]) + (own,)
    step = 0
    for q in range(n_w):
        total = acc_in[q][...] if has_acc else None
        for i in range(n_b):
            if i == n_b - 1 and q == 0:
                load.wait()
            for p in range(PIECES):
                copies[step].wait()
                step += 1
                part = jnp.dot(
                    lhs[i][:, p * piece : (p + 1) * piece],
                    bufs[q][i * feat + p * piece : i * feat + (p + 1) * piece, :],
                    preferred_element_type=F32,
                )
                total = part if total is None else total + part
        outs[q][...] = total


def stream_mm(blocks, masks, weights, accs):
    rows, feat = blocks[0].shape
    ch = weights[0].shape[1]
    n_w = len(weights)
    has_acc = accs is not None
    vm = pl.BlockSpec(memory_space=VMEM)
    depth = feat * len(blocks)
    return pl.pallas_call(
        functools.partial(stream_kernel, masks, n_w, has_acc),
        in_specs=[vm] * (len(blocks) - 1)
        + [pl.BlockSpec(memory_space=pltpu.HBM)]
        + [pl.BlockSpec(memory_space=pltpu.HBM)] * n_w
        + [vm] * (n_w if has_acc else 0),
        out_specs=[vm] * n_w,
        out_shape=[jax.ShapeDtypeStruct((rows, ch), F32)] * n_w,
        scratch_shapes=[VMEM((depth, ch), BF16)] * n_w
        + [pltpu.SemaphoreType.DMA((n_w * len(blocks) * PIECES,))]
        + [VMEM((rows, feat), BF16), pltpu.SemaphoreType.DMA],
        compiler_params=params(12),
        cost_estimate=cost(2 * rows * depth * ch * n_w, 2 * depth * ch * n_w),
    )(*blocks[:-1], far(blocks[-1]), *map(far, weights), *(accs or ()))


def held(value):
    return pltpu.with_memory_space_constraint(value, VMEM)


def mm_kernel(roles, has_acc, edge, *refs):
    n_b = len(roles)
    lhs = refs[:n_b]
    w_ref = refs[n_b]
    total = refs[n_b + 1][...] if has_acc else None
    outs = refs[n_b + 1 + has_acc :]
    feat = lhs[0].shape[1]
    for x, role in zip(lhs, roles):
        at = pl.ds(pl.multiple_of(peer(role) * feat, feat), feat)
        part = jnp.dot(x[...], w_ref[at, :], preferred_element_type=F32)
        total = part if total is None else total + part
    outs[0][...] = total.astype(outs[0].dtype)
    if edge:
        outs[1][...] = total[total.shape[0] - edge :].astype(BF16)


def mm(blocks, roles, weight, acc, edge=0):
    rows, feat = blocks[0].shape
    ch = weight.shape[1]
    vm = pl.BlockSpec(memory_space=VMEM)
    shapes = [jax.ShapeDtypeStruct((rows, ch), BF16 if edge else F32)]
    if edge:
        shapes.append(jax.ShapeDtypeStruct((edge, ch), BF16))
    extra = () if acc is None else (acc,)
    n = len(blocks)
    return pl.pallas_call(
        functools.partial(mm_kernel, roles, len(extra), edge),
        in_specs=[vm] * (n + 1 + len(extra)),
        out_specs=[vm] * len(shapes),
        out_shape=shapes,
        compiler_params=params(5 if n > 5 else 4),
        cost_estimate=cost(2 * n * rows * feat * ch, 2 * n * feat * ch),
    )(*blocks, weight, *extra)


def conv_kernel(split, x_ref, tail_ref, w_ref, b_ref, pw_ref, conv_ref, send_ref, keep_ref, pad, acc):
    rows, ch = x_ref.shape
    taps = w_ref.shape[0]
    edge = tail_ref.shape[0]
    pad[0:edge, :] = tail_ref[...].astype(F32)
    pad[edge : edge + rows, :] = x_ref[...].astype(F32)
    total = jnp.broadcast_to(b_ref[...], (rows, ch))
    for k in range(taps):
        total = total + w_ref[k : k + 1, :] * pad[edge - taps + 1 + k : edge - taps + 1 + k + rows, :]
    conv = (total * jax.nn.sigmoid(total)).astype(BF16)
    conv_ref[...] = conv
    proj = lax.dot_general(conv, pw_ref[...], (((1,), (1,)), ((), ())), preferred_element_type=F32)
    if split:
        half = rows // 2
        core = lax.axis_index("tp") % 2
        acc[...] = proj
        send_ref[...] = acc[pl.ds(pl.multiple_of((1 - core) * half, half), half), :].astype(BF16)
        keep_ref[...] = acc[pl.ds(pl.multiple_of(core * half, half), half), :]
    else:
        keep_ref[...] = proj.astype(keep_ref.dtype)
        send_ref[...] = jnp.zeros(send_ref.shape, send_ref.dtype)


def conv_proj(x, tail, conv_w, conv_b, proj_wt, split):
    rows, ch = x.shape
    wide = proj_wt.shape[0]
    half = rows // 2 if split else rows
    shalf = half if split else 8
    return pl.pallas_call(
        functools.partial(conv_kernel, split),
        in_specs=[pl.BlockSpec(memory_space=VMEM)] * 5,
        out_specs=[pl.BlockSpec(memory_space=VMEM)] * 3,
        out_shape=[
            jax.ShapeDtypeStruct((rows, ch), BF16),
            jax.ShapeDtypeStruct((shalf, wide), BF16),
            jax.ShapeDtypeStruct((half, wide), F32 if split else BF16),
        ],
        scratch_shapes=[VMEM((tail.shape[0] + rows, ch), F32), VMEM((rows, wide), F32)],
        compiler_params=params(6),
        cost_estimate=cost(2 * rows * ch * wide, 2 * ch * wide),
    )(x, tail, conv_w, conv_b, proj_wt)


def spread(ref, value, groups):
    count = value.shape[0]
    for j in range(groups):
        ref[pl.ds(j, count, stride=groups), :] = value[:, j * LANES : (j + 1) * LANES]


def collect(ref, count, groups):
    return jnp.concatenate([ref[pl.ds(j, count, stride=groups), :] for j in range(groups)], axis=1)


def line(ref, at, groups):
    return jnp.broadcast_to(ref[pl.ds(at, 1), :], (groups, LANES))


def scan_kernel(
    split, *refs,
):
    n_p = 2 if split else 1
    parts = refs[:n_p]
    (conv_ref, sw_ref, sb_ref, decay_ref, carried_ref,
     end_ref, pack_ref, y_ref, cum_ref, c_ref,
     proj_s, step_s, drive_s, nd_s, h_s, b_ref) = refs[n_p:]
    rows, ch = conv_ref.shape
    groups = ch // LANES
    if split:
        half = rows // 2
        core = lax.axis_index("tp") % 2
        proj_s[pl.ds(pl.multiple_of(core * half, half), half), :] = parts[0][...].astype(F32)
        proj_s[pl.ds(pl.multiple_of((1 - core) * half, half), half), :] = parts[1][...].astype(F32)
    else:
        proj_s[...] = parts[0][...].astype(F32)
    for n in range(STATE):
        for ref, at in ((b_ref, DT_RANK + n), (c_ref, DT_RANK + STATE + n)):
            ref[pl.ds(n, rows, stride=STATE), :] = jnp.broadcast_to(
                proj_s[:, at : at + 1], (rows, LANES)
            )
    low = proj_s[:, :DT_RANK].astype(BF16)
    pre = jnp.dot(low, sw_ref[...], preferred_element_type=F32) + sb_ref[...]
    step = jnp.maximum(pre, 0.0) + jnp.log1p(jnp.exp(-jnp.abs(pre)))
    spread(step_s, step, groups)
    spread(drive_s, step * conv_ref[...].astype(F32), groups)
    spread(nd_s, decay_ref[...] * -LOG2E, groups)
    lead = jnp.where(lax.axis_index("ctx") == 0, 1.0, 0.0)
    spread(h_s, carried_ref[...] * lead, groups)
    nd = [nd_s[n * groups : (n + 1) * groups, :] for n in range(STATE)]
    h0 = tuple(h_s[n * groups : (n + 1) * groups, :] for n in range(STATE))

    def body(t, carry):
        h, total = carry
        at = pl.ds(pl.multiple_of(t * groups, groups), groups)
        dt = step_s[at, :]
        u = drive_s[at, :]
        total = total + dt
        cum_ref[at, :] = total
        y = None
        new = []
        for n in range(STATE):
            a = jnp.exp2(dt * nd[n])
            v = a * h[n] + u * line(b_ref, t * STATE + n, groups)
            new.append(v)
            term = v * line(c_ref, t * STATE + n, groups)
            y = term if y is None else y + term
        y_ref[at, :] = y
        return tuple(new), total

    h, total = lax.fori_loop(0, rows, body, (h0, jnp.zeros((groups, LANES), F32)), unroll=8)
    for n in range(STATE):
        h_s[n * groups : (n + 1) * groups, :] = h[n]
    end_ref[0:STATE, :] = collect(h_s, STATE, groups)
    nd_s[0:groups, :] = total
    end_ref[STATE : STATE + 1, :] = collect(nd_s, 1, groups)
    pack_ref[...] = end_ref[...].astype(BF16)


def scan(parts, conv_x, step_w, step_b, decay_t, carried_t):
    rows, ch = conv_x.shape
    groups = ch // LANES
    vm = pl.BlockSpec(memory_space=VMEM)
    return pl.pallas_call(
        functools.partial(scan_kernel, len(parts) == 2),
        in_specs=[vm] * (5 + len(parts)),
        out_specs=[vm] * 5,
        out_shape=[
            jax.ShapeDtypeStruct((STATE + 1, ch), F32),
            jax.ShapeDtypeStruct((STATE + 1, ch), BF16),
            jax.ShapeDtypeStruct((rows * groups, LANES), F32),
            jax.ShapeDtypeStruct((rows * groups, LANES), F32),
            jax.ShapeDtypeStruct((rows * STATE, LANES), F32),
        ],
        scratch_shapes=[
            VMEM((rows, parts[0].shape[1]), F32),
            VMEM((rows * groups, LANES), F32),
            VMEM((rows * groups, LANES), F32),
            VMEM((STATE * groups, LANES), F32),
            VMEM((STATE * groups, LANES), F32),
            VMEM((rows * STATE, LANES), F32),
        ],
        compiler_params=params(8),
        cost_estimate=cost(rows * ch * STATE * 8, rows * ch * 8, rows * ch * STATE),
    )(*parts, conv_x, step_w, step_b, decay_t, carried_t)


def add_kernel(*refs):
    total = refs[0][...].astype(F32)
    for r in refs[1:-1]:
        total = total + r[...].astype(F32)
    refs[-1][...] = total.astype(BF16)


def add(*values):
    vm = pl.BlockSpec(memory_space=VMEM)
    shape = values[0].shape
    size = shape[0] * shape[1]
    return pl.pallas_call(
        add_kernel,
        in_specs=[vm] * len(values),
        out_specs=vm,
        out_shape=jax.ShapeDtypeStruct(shape, BF16),
        compiler_params=params(3),
        cost_estimate=cost(size * len(values), 2 * size * len(values)),
    )(*values)


def add_pair_kernel(a_ref, b_ref, *outs):
    for i, o in enumerate(outs):
        o[...] = (a_ref[i].astype(F32) + b_ref[i].astype(F32)).astype(BF16)


def add_pair(a, b):
    vm = pl.BlockSpec(memory_space=VMEM)
    n, rows, feat = a.shape
    return pl.pallas_call(
        add_pair_kernel,
        in_specs=[vm, vm],
        out_specs=[vm] * n,
        out_shape=[jax.ShapeDtypeStruct((rows, feat), BF16)] * n,
        compiler_params=params(3),
        cost_estimate=cost(a.size, 6 * a.size),
    )(a, b)


def merge_kernel(bit, first, last, decay_ref, group_ref, got_ref, *refs):
    ent_ref = None if first else refs[0]
    pack_ref, out_ref = refs[-2:]
    upper = (lax.axis_index("ctx") // bit) % 2 == 1
    decay = decay_ref[...]
    got = got_ref[...].astype(F32)
    gh, gs = got[:STATE], got[STATE:]
    mh, ms = group_ref[:STATE, :], group_ref[STATE:, :]
    entering = gh if first else jnp.exp(-decay * ent_ref[STATE:, :]) * gh + ent_ref[:STATE, :]
    before = gs if first else ent_ref[STATE:, :] + gs
    keep_h = jnp.zeros_like(gh) if first else ent_ref[:STATE, :]
    keep_s = jnp.zeros_like(gs) if first else ent_ref[STATE:, :]
    out_ref[:STATE, :] = jnp.where(upper, entering, keep_h)
    out_ref[STATE:, :] = jnp.where(upper, before, keep_s)
    low = jnp.where(upper, gh, mh)
    high = jnp.where(upper, mh, gh)
    high_s = jnp.where(upper, ms, gs)
    total = jnp.exp(-decay * high_s) * low + high
    pack_ref[:STATE, :] = total.astype(BF16)
    pack_ref[STATE:, :] = (ms + gs).astype(BF16)
    if not last:
        refs[-3][:STATE, :] = total
        refs[-3][STATE:, :] = ms + gs


def merge(bit, decay_t, group, got, ent, last):
    vm = pl.BlockSpec(memory_space=VMEM)
    first = ent is None
    extra = () if first else (ent,)
    return pl.pallas_call(
        functools.partial(merge_kernel, bit, first, last),
        in_specs=[vm] * (3 + len(extra)),
        out_specs=[vm] * (2 if last else 3),
        out_shape=[jax.ShapeDtypeStruct(group.shape, F32)] * (not last)
        + [
            jax.ShapeDtypeStruct(group.shape, BF16),
            jax.ShapeDtypeStruct(group.shape, F32),
        ],
        compiler_params=params(3),
        cost_estimate=cost(group.size * 8, group.size * 16),
    )(decay_t, group, got, *extra)


def gate_kernel(bit, first, y_ref, cum_ref, c_ref, end_ref, got_ref, decay_ref, conv_ref, skip_ref, gate_ref, *refs):
    ent_ref = None if first else refs[0]
    out_ref, bound_ref, nd_s, e_s, y_s = refs[-5:]
    rows, ch = conv_ref.shape
    groups = ch // LANES
    decay = decay_ref[...]
    upper = (lax.axis_index("ctx") // bit) % 2 == 1
    got = got_ref[...].astype(F32)[:STATE]
    if first:
        entering = jnp.where(upper, got, jnp.zeros_like(got))
    else:
        kept = ent_ref[:STATE, :]
        entering = jnp.where(upper, jnp.exp(-decay * ent_ref[STATE:, :]) * got + kept, kept)
    bound_ref[...] = jnp.exp(-decay * end_ref[STATE:, :]) * entering + end_ref[:STATE, :]
    spread(nd_s, decay * -LOG2E, groups)
    spread(e_s, entering, groups)
    nd = [nd_s[n * groups : (n + 1) * groups, :] for n in range(STATE)]
    ent = [e_s[n * groups : (n + 1) * groups, :] for n in range(STATE)]

    def body(t, carry):
        at = pl.ds(pl.multiple_of(t * groups, groups), groups)
        total = cum_ref[at, :]
        y = y_ref[at, :]
        for n in range(STATE):
            y = y + jnp.exp2(total * nd[n]) * ent[n] * line(c_ref, t * STATE + n, groups)
        y_s[at, :] = y
        return carry

    lax.fori_loop(0, rows, body, 0, unroll=8)
    y = collect(y_s, rows, groups)
    gate = gate_ref[...].astype(BF16).astype(F32)
    out = (y + skip_ref[...] * conv_ref[...].astype(F32)) * (gate * jax.nn.sigmoid(gate))
    out_ref[...] = out.astype(BF16)


def gating(bit, y, cum, bc, end, got, ent, decay_t, conv_x, skip, gate):
    rows, ch = conv_x.shape
    groups = ch // LANES
    vm = pl.BlockSpec(memory_space=VMEM)
    first = ent is None
    extra = () if first else (ent,)
    return pl.pallas_call(
        functools.partial(gate_kernel, bit, first),
        in_specs=[vm] * (9 + len(extra)),
        out_specs=[vm, vm],
        out_shape=[
            jax.ShapeDtypeStruct((rows, ch), BF16),
            jax.ShapeDtypeStruct((STATE, ch), F32),
        ],
        scratch_shapes=[
            VMEM((STATE * groups, LANES), F32),
            VMEM((STATE * groups, LANES), F32),
            VMEM((rows * groups, LANES), F32),
        ],
        compiler_params=params(8),
        cost_estimate=cost(rows * ch * STATE * 6, rows * ch * 8, rows * ch * STATE),
    )(y, cum, bc, end, got, decay_t, conv_x, skip, gate, *extra)


def out_stack_kernel(masks, g_ref, w_ref, out):
    feat = out.shape[2]
    for i, mask in enumerate(masks):
        at = pl.ds(pl.multiple_of(peer(mask) * feat, feat), feat)
        out[i] = jnp.dot(g_ref[...], w_ref[:, at], preferred_element_type=F32).astype(BF16)


def out_blocks(gated, weight, masks, feat):
    rows, ch = gated.shape
    n = len(masks)
    vm = pl.BlockSpec(memory_space=VMEM)
    return pl.pallas_call(
        functools.partial(out_stack_kernel, masks),
        in_specs=[vm, vm],
        out_specs=vm,
        out_shape=jax.ShapeDtypeStruct((n, rows, feat), BF16),
        compiler_params=params(4),
        cost_estimate=cost(2 * rows * ch * feat * n, 2 * ch * feat * n),
    )(gated, weight)


def on_device(
    tokens, inner_weight, gate_weight, conv_weight, conv_bias, proj_weight, step_weight,
    step_bias, decay_rate, skip_gain, out_weight, carried_state,
):
    rows, feat = tokens.shape
    n_tp = lax.axis_size("tp")
    n_ctx = lax.axis_size("ctx")
    square = n_tp == 8
    shift = [(i, i + 1) for i in range(n_ctx - 1)]
    proj_wt = proj_weight.T
    decay_t = decay_rate.T
    carried_t = carried_state.T

    if square:
        to_first = [(i, i ^ (2 + 2 * (i % 2))) for i in range(n_tp)]
        to_second = [(i, i ^ (4 - 2 * (i % 2))) for i in range(n_tp)]
        p1 = flip(tokens, "tp", 1)
        vs = lax.ppermute(tokens, "tp", to_second)
        inner, = stream_mm([tokens], [0], [inner_weight], None)
        vf = lax.ppermute(tie(tokens, inner), "tp", to_first)
        vs = tie(vs, inner)
        vd = lax.ppermute(vs, "tp", to_first)
        qs = flip(vs, "tp", 1)
        qf = flip(vf, "tp", 1)
        inner_w, gate_w = held(inner_weight), held(gate_weight)
        inner, = mm([p1, vs, qs, vf, qf], [1, 20, 11, 10, 21], inner_w, inner)
        vd = tie(vd, inner)
        qd = flip(vd, "tp", 1)
        inner_x, edge_x = mm([vd, qd], [6, 7], inner_w, inner, EDGE)
    else:
        piece = lax.all_gather(tokens, "tp", axis=1, tiled=True)
        inner_x = jnp.dot(piece, inner_weight, preferred_element_type=F32).astype(BF16)
        gate_acc = jnp.dot(piece, gate_weight, preferred_element_type=F32)
        edge_x = inner_x[rows - EDGE :]

    tail = lax.ppermute(edge_x, "ctx", shift)
    conv_x, send, keep = conv_proj(
        inner_x, tail, conv_weight, conv_bias[None, :], proj_wt, square
    )
    if square:
        part = add(keep, flip(send, "tp", 1))
        quarter = [flip(part, "tp", m) for m in (2, 4, 6)]
        blocks = [tokens, p1, vs, qs, vf, qf, vd, qd]
        gate_acc, = mm(
            [tie(tokens, part), *blocks[1:]], [0, 1, 20, 11, 10, 21, 6, 7], gate_w, None
        )
        quarter = [tie(v, gate_acc) for v in quarter]
        mine = add(part, *quarter)
        parts = (mine, flip(mine, "tp", 1))
    else:
        parts = (lax.psum(keep, "tp"),)
    end, packet, y, cum, bc = scan(
        parts, conv_x, step_weight, step_bias[None, :], decay_t, carried_t
    )

    group, ent, bit = end, None, 1
    while bit * 2 < n_ctx:
        got = flip(packet, "ctx", bit)
        *group, packet, ent = merge(bit, decay_t, group, got, ent, bit * 4 >= n_ctx)
        group = group[0] if group else None
        bit *= 2
    got = flip(packet, "ctx", bit)
    gated, bound = gating(
        bit, y, cum, bc, end, got, ent, decay_t, conv_x, skip_gain[None, :], gate_acc
    )
    if square:
        out_weight = pltpu.with_memory_space_constraint(out_weight, VMEM)
        away = out_blocks(gated, out_weight, [7, 21], feat)
        got = flip(away, "tp", 1)
        away_b = out_blocks(gated, out_weight, [11, 1], feat)
        got_b = flip(away_b, "tp", 1)
        near = out_blocks(gated, out_weight, [6, 10], feat)
        sd, sf = add_pair(near, got)
        near_b = out_blocks(gated, out_weight, [20, 0], feat)
        ss, so = add_pair(near_b, got_b)
        rd = lax.ppermute(sd, "tp", to_first)
        rf = lax.ppermute(sf, "tp", to_first)
        rs = lax.ppermute(add(ss, rd), "tp", to_second)
        mixed = add(so, rf, rs)
    else:
        partial = jnp.dot(gated, out_weight, preferred_element_type=F32).astype(BF16)
        mixed = lax.psum_scatter(partial, "tp", scatter_dimension=1, tiled=True)
    return (mixed, bound.T[None])


def solution(mesh):
    in_specs = (
        P("ctx", "tp"), P(None, "tp"), P(None, "tp"), P(None, "tp"), P("tp"), P("tp", None),
        P(None, "tp"), P("tp"), P("tp", None), P("tp"), P("tp", None), P("tp", None),
    )
    out_specs = (P("ctx", "tp"), P("ctx", "tp", None))
    return jax.shard_map(
        on_device, mesh=mesh, in_specs=in_specs, out_specs=out_specs, check_vma=False
    )
```

```python
import functools
import math

import jax
import jax.numpy as jnp
from jax import lax
from jax.experimental import pallas as pl
from jax.experimental.pallas import tpu as pltpu
from jax.sharding import PartitionSpec as P


STATE = 16
DT_RANK = 512
LANES = 128
EDGE = 8
LOG2E = math.log2(math.e)
F32 = jnp.float32
BF16 = jnp.bfloat16
VMEM = pltpu.VMEM


def flip(value, axis, mask):
    peers = lax.axis_size(axis)
    return lax.ppermute(value, axis, [(i, i ^ mask) for i in range(peers)])


def cost(flops, nbytes, trans=0):
    return pl.CostEstimate(flops=flops, bytes_accessed=nbytes, transcendentals=trans)


PIECES = 2


def params(mib):
    return pltpu.CompilerParams(vmem_limit_bytes=mib << 20)


def far(value):
    return pltpu.with_memory_space_constraint(value, pltpu.HBM)


def tie(value, *others):
    return lax.optimization_barrier((value, *others))[0]


def peer(role):
    me = lax.axis_index("tp")
    core = me % 2
    if role >= 20:
        return me ^ (4 - 2 * core) ^ (role - 20)
    if role >= 10:
        return me ^ (2 + 2 * core) ^ (role - 10)
    return me ^ role


def row_copies(masks, weights, bufs, sem, feat):
    copies = []
    piece = feat // PIECES
    for q, (w, buf) in enumerate(zip(weights, bufs)):
        for i, mask in enumerate(masks):
            for p in range(PIECES):
                at = pl.multiple_of((peer(mask)) * feat + p * piece, piece)
                copies.append(
                    pltpu.make_async_copy(
                        w.at[pl.ds(at, piece), :],
                        buf.at[pl.ds(i * feat + p * piece, piece), :],
                        sem.at[(q * len(masks) + i) * PIECES + p],
                    )
                )
    return copies


def stream_kernel(masks, n_w, has_acc, *refs):
    n_b = len(masks)
    lhs = refs[:n_b]
    w = refs[n_b : n_b + n_w]
    refs = refs[n_b + n_w :]
    acc_in = refs[:n_w] if has_acc else None
    refs = refs[n_w:] if has_acc else refs
    outs = refs[:n_w]
    bufs = refs[n_w : 2 * n_w]
    sem = refs[2 * n_w]
    feat = lhs[0].shape[1]
    piece = feat // PIECES
    copies = row_copies(masks, w, bufs, sem, feat)
    own, own_sem = refs[2 * n_w + 1 :]
    load = pltpu.make_async_copy(lhs[-1], own, own_sem)
    load.start()
    for c in copies:
        c.start()
    lhs = tuple(lhs[:-1]) + (own,)
    step = 0
    for q in range(n_w):
        total = acc_in[q][...] if has_acc else None
        for i in range(n_b):
            if i == n_b - 1 and q == 0:
                load.wait()
            for p in range(PIECES):
                copies[step].wait()
                step += 1
                part = jnp.dot(
                    lhs[i][:, p * piece : (p + 1) * piece],
                    bufs[q][i * feat + p * piece : i * feat + (p + 1) * piece, :],
                    preferred_element_type=F32,
                )
                total = part if total is None else total + part
        outs[q][...] = total


def stream_mm(blocks, masks, weights, accs):
    rows, feat = blocks[0].shape
    ch = weights[0].shape[1]
    n_w = len(weights)
    has_acc = accs is not None
    vm = pl.BlockSpec(memory_space=VMEM)
    depth = feat * len(blocks)
    return pl.pallas_call(
        functools.partial(stream_kernel, masks, n_w, has_acc),
        in_specs=[vm] * (len(blocks) - 1)
        + [pl.BlockSpec(memory_space=pltpu.HBM)]
        + [pl.BlockSpec(memory_space=pltpu.HBM)] * n_w
        + [vm] * (n_w if has_acc else 0),
        out_specs=[vm] * n_w,
        out_shape=[jax.ShapeDtypeStruct((rows, ch), F32)] * n_w,
        scratch_shapes=[VMEM((depth, ch), BF16)] * n_w
        + [pltpu.SemaphoreType.DMA((n_w * len(blocks) * PIECES,))]
        + [VMEM((rows, feat), BF16), pltpu.SemaphoreType.DMA],
        compiler_params=params(12),
        cost_estimate=cost(2 * rows * depth * ch * n_w, 2 * depth * ch * n_w),
    )(*blocks[:-1], far(blocks[-1]), *map(far, weights), *(accs or ()))


def held(value):
    return pltpu.with_memory_space_constraint(value, VMEM)


def mm_kernel(roles, has_acc, edge, *refs):
    n_b = len(roles)
    lhs = refs[:n_b]
    w_ref = refs[n_b]
    total = refs[n_b + 1][...] if has_acc else None
    outs = refs[n_b + 1 + has_acc :]
    feat = lhs[0].shape[1]
    for x, role in zip(lhs, roles):
        at = pl.ds(pl.multiple_of(peer(role) * feat, feat), feat)
        part = jnp.dot(x[...], w_ref[at, :], preferred_element_type=F32)
        total = part if total is None else total + part
    outs[0][...] = total.astype(outs[0].dtype)
    if edge:
        outs[1][...] = total[total.shape[0] - edge :].astype(BF16)


def mm(blocks, roles, weight, acc, edge=0):
    rows, feat = blocks[0].shape
    ch = weight.shape[1]
    vm = pl.BlockSpec(memory_space=VMEM)
    shapes = [jax.ShapeDtypeStruct((rows, ch), BF16 if edge else F32)]
    if edge:
        shapes.append(jax.ShapeDtypeStruct((edge, ch), BF16))
    extra = () if acc is None else (acc,)
    n = len(blocks)
    return pl.pallas_call(
        functools.partial(mm_kernel, roles, len(extra), edge),
        in_specs=[vm] * (n + 1 + len(extra)),
        out_specs=[vm] * len(shapes),
        out_shape=shapes,
        compiler_params=params(5 if n > 5 else 4),
        cost_estimate=cost(2 * n * rows * feat * ch, 2 * n * feat * ch),
    )(*blocks, weight, *extra)


def convolve(pad, w_ref, b_ref, edge, rows):
    taps = w_ref.shape[0]
    total = jnp.broadcast_to(b_ref[...], (rows, b_ref.shape[1]))
    for k in range(taps):
        at = edge - taps + 1 + k
        total = total + w_ref[k : k + 1, :] * pad[at : at + rows, :]
    return (total * jax.nn.sigmoid(total)).astype(BF16)


def project(conv, pw_ref):
    return lax.dot_general(conv, pw_ref[...], (((1,), (1,)), ((), ())), preferred_element_type=F32)


def conv_kernel(x_ref, w_ref, b_ref, pw_ref, conv_ref, proj_ref, pad):
    rows, ch = x_ref.shape
    pad[0:EDGE, :] = jnp.zeros((EDGE, ch), F32)
    pad[EDGE : EDGE + rows, :] = x_ref[...].astype(F32)
    conv = convolve(pad, w_ref, b_ref, EDGE, rows)
    conv_ref[...] = conv
    proj_ref[...] = project(conv, pw_ref)


def head_kernel(split, x_ref, tail_ref, w_ref, b_ref, pw_ref, conv0_ref, proj0_ref, conv_ref, send_ref, keep_ref, pad, acc):
    rows = x_ref.shape[0]
    head = pad.shape[0] - EDGE
    pad[0:EDGE, :] = tail_ref[...].astype(F32)
    pad[EDGE:, :] = x_ref[0:head, :].astype(F32)
    conv = convolve(pad, w_ref, b_ref, EDGE, head)
    conv_ref[...] = conv0_ref[...]
    conv_ref[0:head, :] = conv
    acc[...] = proj0_ref[...]
    acc[0:head, :] = project(conv, pw_ref)
    if split:
        half = rows // 2
        core = lax.axis_index("tp") % 2
        send_ref[...] = acc[pl.ds(pl.multiple_of((1 - core) * half, half), half), :].astype(BF16)
        keep_ref[...] = acc[pl.ds(pl.multiple_of(core * half, half), half), :]
    else:
        keep_ref[...] = acc[...].astype(keep_ref.dtype)
        send_ref[...] = jnp.zeros(send_ref.shape, send_ref.dtype)


def conv_proj(x, conv_w, conv_b, proj_wt):
    rows, ch = x.shape
    wide = proj_wt.shape[0]
    vm = pl.BlockSpec(memory_space=VMEM)
    return pl.pallas_call(
        conv_kernel,
        in_specs=[vm] * 4,
        out_specs=[vm] * 2,
        out_shape=[
            jax.ShapeDtypeStruct((rows, ch), BF16),
            jax.ShapeDtypeStruct((rows, wide), F32),
        ],
        scratch_shapes=[VMEM((EDGE + rows, ch), F32)],
        compiler_params=params(6),
        cost_estimate=cost(2 * rows * ch * wide, 2 * ch * wide),
    )(x, conv_w, conv_b, proj_wt)


def conv_head(x, tail, conv_w, conv_b, proj_wt, conv0, proj0, split):
    rows, ch = x.shape
    wide = proj_wt.shape[0]
    head = min(2 * EDGE, rows)
    half = rows // 2 if split else rows
    vm = pl.BlockSpec(memory_space=VMEM)
    return pl.pallas_call(
        functools.partial(head_kernel, split),
        in_specs=[vm] * 7,
        out_specs=[vm] * 3,
        out_shape=[
            jax.ShapeDtypeStruct((rows, ch), BF16),
            jax.ShapeDtypeStruct((half if split else EDGE, wide), BF16),
            jax.ShapeDtypeStruct((half, wide), F32 if split else BF16),
        ],
        scratch_shapes=[VMEM((EDGE + head, ch), F32), VMEM((rows, wide), F32)],
        compiler_params=params(4),
        cost_estimate=cost(2 * head * ch * wide, 2 * ch * wide),
    )(x, tail, conv_w, conv_b, proj_wt, conv0, proj0)


def spread(ref, value, groups):
    count = value.shape[0]
    for j in range(groups):
        ref[pl.ds(j, count, stride=groups), :] = value[:, j * LANES : (j + 1) * LANES]


def collect(ref, count, groups):
    return jnp.concatenate([ref[pl.ds(j, count, stride=groups), :] for j in range(groups)], axis=1)


def across(ref, bc_ref, first):
    rows = bc_ref.shape[0]
    for n in range(STATE):
        ref[pl.ds(n, rows, stride=STATE), :] = jnp.broadcast_to(
            bc_ref[:, first + n : first + n + 1], (rows, LANES)
        )


def line(ref, at, groups):
    return jnp.broadcast_to(ref[pl.ds(at, 1), :], (groups, LANES))


def scan_kernel(
    split, *refs,
):
    n_p = 2 if split else 1
    parts = refs[:n_p]
    (conv_ref, sw_ref, sb_ref, decay_ref, carried_ref,
     end_ref, pack_ref, step_s, drive_s, b_ref, bc_ref,
     proj_s, nd_s, h_s) = refs[n_p:]
    rows, ch = conv_ref.shape
    groups = ch // LANES
    if split:
        half = rows // 2
        core = lax.axis_index("tp") % 2
        proj_s[pl.ds(pl.multiple_of(core * half, half), half), :] = parts[0][...].astype(F32)
        proj_s[pl.ds(pl.multiple_of((1 - core) * half, half), half), :] = parts[1][...].astype(F32)
    else:
        proj_s[...] = parts[0][...].astype(F32)
    bc_ref[...] = proj_s[:, DT_RANK:]
    across(b_ref, bc_ref, 0)
    low = proj_s[:, :DT_RANK].astype(BF16)
    pre = jnp.dot(low, sw_ref[...], preferred_element_type=F32) + sb_ref[...]
    step = jnp.maximum(pre, 0.0) + jnp.log1p(jnp.exp(-jnp.abs(pre)))
    spread(step_s, step, groups)
    spread(drive_s, step * conv_ref[...].astype(F32), groups)
    spread(nd_s, decay_ref[...] * -LOG2E, groups)
    lead = jnp.where(lax.axis_index("ctx") == 0, 1.0, 0.0)
    spread(h_s, carried_ref[...] * lead, groups)
    nd = [nd_s[n * groups : (n + 1) * groups, :] for n in range(STATE)]
    h0 = tuple(h_s[n * groups : (n + 1) * groups, :] for n in range(STATE))

    def body(t, carry):
        h, total = carry
        at = pl.ds(pl.multiple_of(t * groups, groups), groups)
        dt = step_s[at, :]
        u = drive_s[at, :]
        new = tuple(
            jnp.exp2(dt * nd[n]) * h[n] + u * line(b_ref, t * STATE + n, groups)
            for n in range(STATE)
        )
        return new, total + dt

    h, total = lax.fori_loop(0, rows, body, (h0, jnp.zeros((groups, LANES), F32)), unroll=8)
    for n in range(STATE):
        h_s[n * groups : (n + 1) * groups, :] = h[n]
    end_ref[0:STATE, :] = collect(h_s, STATE, groups)
    nd_s[0:groups, :] = total
    end_ref[STATE : STATE + 1, :] = collect(nd_s, 1, groups)
    pack_ref[...] = end_ref[...].astype(BF16)


def scan(parts, conv_x, step_w, step_b, decay_t, carried_t):
    rows, ch = conv_x.shape
    groups = ch // LANES
    vm = pl.BlockSpec(memory_space=VMEM)
    return pl.pallas_call(
        functools.partial(scan_kernel, len(parts) == 2),
        in_specs=[vm] * (5 + len(parts)),
        out_specs=[vm] * 6,
        out_shape=[
            jax.ShapeDtypeStruct((STATE + 1, ch), F32),
            jax.ShapeDtypeStruct((STATE + 1, ch), BF16),
            jax.ShapeDtypeStruct((rows * groups, LANES), F32),
            jax.ShapeDtypeStruct((rows * groups, LANES), F32),
            jax.ShapeDtypeStruct((rows * STATE, LANES), F32),
            jax.ShapeDtypeStruct((rows, 2 * STATE), F32),
        ],
        scratch_shapes=[
            VMEM((rows, parts[0].shape[1]), F32),
            VMEM((STATE * groups, LANES), F32),
            VMEM((STATE * groups, LANES), F32),
        ],
        compiler_params=params(8),
        cost_estimate=cost(rows * ch * STATE * 8, rows * ch * 8, rows * ch * STATE),
    )(*parts, conv_x, step_w, step_b, decay_t, carried_t)


def local_kernel(step_ref, drive_ref, b_ref, bc_ref, decay_ref, carried_ref, y_ref, cum_ref, c_ref, nd_s, h_s):
    across(c_ref, bc_ref, STATE)
    groups = decay_ref.shape[1] // LANES
    rows = step_ref.shape[0] // groups
    spread(nd_s, decay_ref[...] * -LOG2E, groups)
    lead = jnp.where(lax.axis_index("ctx") == 0, 1.0, 0.0)
    spread(h_s, carried_ref[...] * lead, groups)
    nd = [nd_s[n * groups : (n + 1) * groups, :] for n in range(STATE)]
    h0 = tuple(h_s[n * groups : (n + 1) * groups, :] for n in range(STATE))

    def body(t, carry):
        h, total = carry
        at = pl.ds(pl.multiple_of(t * groups, groups), groups)
        dt = step_ref[at, :]
        u = drive_ref[at, :]
        total = total + dt
        cum_ref[at, :] = total
        y = None
        new = []
        for n in range(STATE):
            v = jnp.exp2(dt * nd[n]) * h[n] + u * line(b_ref, t * STATE + n, groups)
            new.append(v)
            term = v * line(c_ref, t * STATE + n, groups)
            y = term if y is None else y + term
        y_ref[at, :] = y
        return tuple(new), total

    lax.fori_loop(0, rows, body, (h0, jnp.zeros((groups, LANES), F32)), unroll=8)


def local_readout(step, drive, b, bc, decay_t, carried_t):
    groups = decay_t.shape[1] // LANES
    vm = pl.BlockSpec(memory_space=VMEM)
    return pl.pallas_call(
        local_kernel,
        in_specs=[vm] * 6,
        out_specs=[vm] * 3,
        out_shape=[jax.ShapeDtypeStruct(step.shape, F32)] * 2
        + [jax.ShapeDtypeStruct(b.shape, F32)],
        scratch_shapes=[VMEM((STATE * groups, LANES), F32)] * 2,
        compiler_params=params(4),
        cost_estimate=cost(step.size * STATE * 8, step.size * 16, step.size * STATE),
    )(step, drive, b, bc, decay_t, carried_t)


def weight_kernel(cum_ref, c_ref, decay_ref, q_ref, nd_s):
    groups = decay_ref.shape[1] // LANES
    rows = cum_ref.shape[0] // groups
    spread(nd_s, decay_ref[...] * -LOG2E, groups)
    nd = [nd_s[n * groups : (n + 1) * groups, :] for n in range(STATE)]

    def body(t, carry):
        total = cum_ref[pl.ds(pl.multiple_of(t * groups, groups), groups), :]
        for n in range(STATE):
            at = pl.ds(pl.multiple_of((t * STATE + n) * groups, groups), groups)
            q_ref[at, :] = jnp.exp2(total * nd[n]) * line(c_ref, t * STATE + n, groups)
        return carry

    lax.fori_loop(0, rows, body, 0, unroll=4)


def weights(cum, c, decay_t):
    groups = decay_t.shape[1] // LANES
    vm = pl.BlockSpec(memory_space=VMEM)
    return pl.pallas_call(
        weight_kernel,
        in_specs=[vm] * 3,
        out_specs=vm,
        out_shape=jax.ShapeDtypeStruct((cum.shape[0] * STATE, LANES), F32),
        scratch_shapes=[VMEM((STATE * groups, LANES), F32)],
        compiler_params=params(2),
        cost_estimate=cost(cum.size * STATE * 3, cum.size * 4, cum.size * STATE),
    )(cum, c, decay_t)


def add_kernel(*refs):
    total = refs[0][...].astype(F32)
    for r in refs[1:-1]:
        total = total + r[...].astype(F32)
    refs[-1][...] = total.astype(BF16)


def add(*values):
    vm = pl.BlockSpec(memory_space=VMEM)
    shape = values[0].shape
    size = shape[0] * shape[1]
    return pl.pallas_call(
        add_kernel,
        in_specs=[vm] * len(values),
        out_specs=vm,
        out_shape=jax.ShapeDtypeStruct(shape, BF16),
        compiler_params=params(3),
        cost_estimate=cost(size * len(values), 2 * size * len(values)),
    )(*values)


def add_pair_kernel(a_ref, b_ref, *outs):
    for i, o in enumerate(outs):
        o[...] = (a_ref[i].astype(F32) + b_ref[i].astype(F32)).astype(BF16)


def add_pair(a, b):
    vm = pl.BlockSpec(memory_space=VMEM)
    n, rows, feat = a.shape
    return pl.pallas_call(
        add_pair_kernel,
        in_specs=[vm, vm],
        out_specs=[vm] * n,
        out_shape=[jax.ShapeDtypeStruct((rows, feat), BF16)] * n,
        compiler_params=params(3),
        cost_estimate=cost(a.size, 6 * a.size),
    )(a, b)


def merge_kernel(bit, first, last, decay_ref, group_ref, got_ref, *refs):
    ent_ref = None if first else refs[0]
    pack_ref, out_ref = refs[-2:]
    upper = (lax.axis_index("ctx") // bit) % 2 == 1
    decay = decay_ref[...]
    got = got_ref[...].astype(F32)
    gh, gs = got[:STATE], got[STATE:]
    mh, ms = group_ref[:STATE, :], group_ref[STATE:, :]
    entering = gh if first else jnp.exp(-decay * ent_ref[STATE:, :]) * gh + ent_ref[:STATE, :]
    before = gs if first else ent_ref[STATE:, :] + gs
    keep_h = jnp.zeros_like(gh) if first else ent_ref[:STATE, :]
    keep_s = jnp.zeros_like(gs) if first else ent_ref[STATE:, :]
    out_ref[:STATE, :] = jnp.where(upper, entering, keep_h)
    out_ref[STATE:, :] = jnp.where(upper, before, keep_s)
    low = jnp.where(upper, gh, mh)
    high = jnp.where(upper, mh, gh)
    high_s = jnp.where(upper, ms, gs)
    total = jnp.exp(-decay * high_s) * low + high
    pack_ref[:STATE, :] = total.astype(BF16)
    pack_ref[STATE:, :] = (ms + gs).astype(BF16)
    if not last:
        refs[-3][:STATE, :] = total
        refs[-3][STATE:, :] = ms + gs


def merge(bit, decay_t, group, got, ent, last):
    vm = pl.BlockSpec(memory_space=VMEM)
    first = ent is None
    extra = () if first else (ent,)
    return pl.pallas_call(
        functools.partial(merge_kernel, bit, first, last),
        in_specs=[vm] * (3 + len(extra)),
        out_specs=[vm] * (2 if last else 3),
        out_shape=[jax.ShapeDtypeStruct(group.shape, F32)] * (not last)
        + [
            jax.ShapeDtypeStruct(group.shape, BF16),
            jax.ShapeDtypeStruct(group.shape, F32),
        ],
        compiler_params=params(3),
        cost_estimate=cost(group.size * 8, group.size * 16),
    )(decay_t, group, got, *extra)


def gate_kernel(bit, first, y_ref, q_ref, end_ref, got_ref, decay_ref, conv_ref, skip_ref, gate_ref, *refs):
    ent_ref = None if first else refs[0]
    out_ref, bound_ref, e_s, y_s = refs[-4:]
    rows, ch = conv_ref.shape
    groups = ch // LANES
    decay = decay_ref[...]
    upper = (lax.axis_index("ctx") // bit) % 2 == 1
    got = got_ref[...].astype(F32)[:STATE]
    if first:
        entering = jnp.where(upper, got, jnp.zeros_like(got))
    else:
        kept = ent_ref[:STATE, :]
        entering = jnp.where(upper, jnp.exp(-decay * ent_ref[STATE:, :]) * got + kept, kept)
    bound_ref[...] = jnp.exp(-decay * end_ref[STATE:, :]) * entering + end_ref[:STATE, :]
    spread(e_s, entering, groups)
    ent = [e_s[n * groups : (n + 1) * groups, :] for n in range(STATE)]

    def body(t, carry):
        at = pl.ds(pl.multiple_of(t * groups, groups), groups)
        y = y_ref[at, :]
        for n in range(STATE):
            y = y + q_ref[pl.ds(pl.multiple_of((t * STATE + n) * groups, groups), groups), :] * ent[n]
        y_s[at, :] = y
        return carry

    lax.fori_loop(0, rows, body, 0, unroll=8)
    y = collect(y_s, rows, groups)
    gate = gate_ref[...].astype(BF16).astype(F32)
    out = (y + skip_ref[...] * conv_ref[...].astype(F32)) * (gate * jax.nn.sigmoid(gate))
    out_ref[...] = out.astype(BF16)


def gating(bit, y, q, end, got, ent, decay_t, conv_x, skip, gate):
    rows, ch = conv_x.shape
    groups = ch // LANES
    vm = pl.BlockSpec(memory_space=VMEM)
    first = ent is None
    extra = () if first else (ent,)
    return pl.pallas_call(
        functools.partial(gate_kernel, bit, first),
        in_specs=[vm] * (8 + len(extra)),
        out_specs=[vm, vm],
        out_shape=[
            jax.ShapeDtypeStruct((rows, ch), BF16),
            jax.ShapeDtypeStruct((STATE, ch), F32),
        ],
        scratch_shapes=[
            VMEM((STATE * groups, LANES), F32),
            VMEM((rows * groups, LANES), F32),
        ],
        compiler_params=params(8),
        cost_estimate=cost(rows * ch * STATE * 6, rows * ch * 8, rows * ch * STATE),
    )(y, q, end, got, decay_t, conv_x, skip, gate, *extra)


def out_stack_kernel(masks, g_ref, w_ref, out):
    feat = out.shape[2]
    for i, mask in enumerate(masks):
        at = pl.ds(pl.multiple_of(peer(mask) * feat, feat), feat)
        out[i] = jnp.dot(g_ref[...], w_ref[:, at], preferred_element_type=F32).astype(BF16)


def out_blocks(gated, weight, masks, feat):
    rows, ch = gated.shape
    n = len(masks)
    vm = pl.BlockSpec(memory_space=VMEM)
    return pl.pallas_call(
        functools.partial(out_stack_kernel, masks),
        in_specs=[vm, vm],
        out_specs=vm,
        out_shape=jax.ShapeDtypeStruct((n, rows, feat), BF16),
        compiler_params=params(4),
        cost_estimate=cost(2 * rows * ch * feat * n, 2 * ch * feat * n),
    )(gated, weight)


def on_device(
    tokens, inner_weight, gate_weight, conv_weight, conv_bias, proj_weight, step_weight,
    step_bias, decay_rate, skip_gain, out_weight, carried_state,
):
    rows, feat = tokens.shape
    n_tp = lax.axis_size("tp")
    n_ctx = lax.axis_size("ctx")
    square = n_tp == 8
    shift = [(i, i + 1) for i in range(n_ctx - 1)]
    proj_wt = proj_weight.T
    decay_t = decay_rate.T
    carried_t = carried_state.T

    if square:
        to_first = [(i, i ^ (2 + 2 * (i % 2))) for i in range(n_tp)]
        to_second = [(i, i ^ (4 - 2 * (i % 2))) for i in range(n_tp)]
        p1 = flip(tokens, "tp", 1)
        vs = lax.ppermute(tokens, "tp", to_second)
        inner, = stream_mm([tokens], [0], [inner_weight], None)
        vf = lax.ppermute(tie(tokens, inner), "tp", to_first)
        vs = tie(vs, inner)
        vd = lax.ppermute(vs, "tp", to_first)
        qs = flip(vs, "tp", 1)
        qf = flip(vf, "tp", 1)
        inner_w, gate_w = held(inner_weight), held(gate_weight)
        inner, = mm([p1, vs, qs, vf, qf], [1, 20, 11, 10, 21], inner_w, inner)
        vd = tie(vd, inner)
        qd = flip(vd, "tp", 1)
        inner, = mm([vd], [6], inner_w, inner)
        qd = tie(qd, inner)
        inner_x, edge_x = mm([qd], [7], inner_w, inner, EDGE)
    else:
        piece = lax.all_gather(tokens, "tp", axis=1, tiled=True)
        inner_x = jnp.dot(piece, inner_weight, preferred_element_type=F32).astype(BF16)
        gate_acc = jnp.dot(piece, gate_weight, preferred_element_type=F32)
        edge_x = inner_x[rows - EDGE :]

    tail = lax.ppermute(edge_x, "ctx", shift)
    conv_b = conv_bias[None, :]
    conv0, proj0 = conv_proj(inner_x, conv_weight, conv_b, proj_wt)
    conv_x, send, keep = conv_head(
        inner_x, tie(tail, proj0), conv_weight, conv_b, proj_wt, conv0, proj0, square
    )
    if square:
        part = add(keep, flip(send, "tp", 1))
        quarter = [flip(part, "tp", m) for m in (2, 4, 6)]
        blocks = [tokens, p1, vs, qs, vf, qf, vd, qd]
        gate_acc, = mm(
            [tie(tokens, part), *blocks[1:]], [0, 1, 20, 11, 10, 21, 6, 7], gate_w, None
        )
        quarter = [tie(v, gate_acc) for v in quarter]
        mine = add(part, *quarter)
        parts = (mine, flip(mine, "tp", 1))
    else:
        parts = (lax.psum(keep, "tp"),)
    end, packet, step, drive, b_rows, bc = scan(
        parts, conv_x, step_weight, step_bias[None, :], decay_t, carried_t
    )

    y, cum, c_rows = local_readout(step, drive, b_rows, bc, decay_t, carried_t)
    group, ent, bit = end, None, 1
    while bit * 2 < n_ctx:
        got = flip(packet, "ctx", bit)
        if bit == 1:
            got = tie(got, y)
        *group, packet, ent = merge(bit, decay_t, group, got, ent, bit * 4 >= n_ctx)
        group = group[0] if group else None
        bit *= 2
    got = flip(packet, "ctx", bit)
    q = weights(cum, c_rows, tie(decay_t, packet))
    got = tie(got, q)
    gated, bound = gating(
        bit, y, q, end, got, ent, decay_t, conv_x, skip_gain[None, :], gate_acc
    )
    if square:
        out_weight = pltpu.with_memory_space_constraint(out_weight, VMEM)
        away = out_blocks(gated, out_weight, [7, 21], feat)
        got = flip(away, "tp", 1)
        away_b = out_blocks(gated, out_weight, [11, 1], feat)
        got_b = flip(away_b, "tp", 1)
        near = out_blocks(gated, out_weight, [6, 10], feat)
        sd, sf = add_pair(near, got)
        near_b = out_blocks(gated, out_weight, [20, 0], feat)
        ss, so = add_pair(near_b, got_b)
        rd = lax.ppermute(sd, "tp", to_first)
        rf = lax.ppermute(sf, "tp", to_first)
        rs = lax.ppermute(add(ss, rd), "tp", to_second)
        mixed = add(so, rf, rs)
    else:
        partial = jnp.dot(gated, out_weight, preferred_element_type=F32).astype(BF16)
        mixed = lax.psum_scatter(partial, "tp", scatter_dimension=1, tiled=True)
    return (mixed, bound.T[None])


def solution(mesh):
    in_specs = (
        P("ctx", "tp"), P(None, "tp"), P(None, "tp"), P(None, "tp"), P("tp"), P("tp", None),
        P(None, "tp"), P("tp"), P("tp", None), P("tp"), P("tp", None), P("tp", None),
    )
    out_specs = (P("ctx", "tp"), P("ctx", "tp", None))
    return jax.shard_map(
        on_device, mesh=mesh, in_specs=in_specs, out_specs=out_specs, check_vma=False
    )
```

```python
import functools
import math

import jax
import jax.numpy as jnp
from jax import lax
from jax.experimental import pallas as pl
from jax.experimental.pallas import tpu as pltpu
from jax.sharding import PartitionSpec as P


STATE = 16
DT_RANK = 512
LANES = 128
EDGE = 8
LOG2E = math.log2(math.e)
F32 = jnp.float32
BF16 = jnp.bfloat16
VMEM = pltpu.VMEM


def flip(value, axis, mask):
    peers = lax.axis_size(axis)
    return lax.ppermute(value, axis, [(i, i ^ mask) for i in range(peers)])


def cost(flops, nbytes, trans=0):
    return pl.CostEstimate(flops=flops, bytes_accessed=nbytes, transcendentals=trans)


PIECES = 2


def params(mib):
    return pltpu.CompilerParams(vmem_limit_bytes=mib << 20)


def far(value):
    return pltpu.with_memory_space_constraint(value, pltpu.HBM)


def tie(value, *others):
    return lax.optimization_barrier((value, *others))[0]


def peer(role):
    me = lax.axis_index("tp")
    core = me % 2
    if role >= 20:
        return me ^ (4 - 2 * core) ^ (role - 20)
    if role >= 10:
        return me ^ (2 + 2 * core) ^ (role - 10)
    return me ^ role


def row_copies(masks, weights, bufs, sem, feat):
    copies = []
    piece = feat // PIECES
    for q, (w, buf) in enumerate(zip(weights, bufs)):
        for i, mask in enumerate(masks):
            for p in range(PIECES):
                at = pl.multiple_of((peer(mask)) * feat + p * piece, piece)
                copies.append(
                    pltpu.make_async_copy(
                        w.at[pl.ds(at, piece), :],
                        buf.at[pl.ds(i * feat + p * piece, piece), :],
                        sem.at[(q * len(masks) + i) * PIECES + p],
                    )
                )
    return copies


def stream_kernel(masks, n_w, has_acc, *refs):
    n_b = len(masks)
    lhs = refs[:n_b]
    w = refs[n_b : n_b + n_w]
    refs = refs[n_b + n_w :]
    acc_in = refs[:n_w] if has_acc else None
    refs = refs[n_w:] if has_acc else refs
    outs = refs[:n_w]
    bufs = refs[n_w : 2 * n_w]
    sem = refs[2 * n_w]
    feat = lhs[0].shape[1]
    piece = feat // PIECES
    copies = row_copies(masks, w, bufs, sem, feat)
    own, own_sem = refs[2 * n_w + 1 :]
    load = pltpu.make_async_copy(lhs[-1], own, own_sem)
    load.start()
    for c in copies:
        c.start()
    lhs = tuple(lhs[:-1]) + (own,)
    step = 0
    for q in range(n_w):
        total = acc_in[q][...] if has_acc else None
        for i in range(n_b):
            if i == n_b - 1 and q == 0:
                load.wait()
            for p in range(PIECES):
                copies[step].wait()
                step += 1
                part = jnp.dot(
                    lhs[i][:, p * piece : (p + 1) * piece],
                    bufs[q][i * feat + p * piece : i * feat + (p + 1) * piece, :],
                    preferred_element_type=F32,
                )
                total = part if total is None else total + part
        outs[q][...] = total


def stream_mm(blocks, masks, weights, accs):
    rows, feat = blocks[0].shape
    ch = weights[0].shape[1]
    n_w = len(weights)
    has_acc = accs is not None
    vm = pl.BlockSpec(memory_space=VMEM)
    depth = feat * len(blocks)
    return pl.pallas_call(
        functools.partial(stream_kernel, masks, n_w, has_acc),
        in_specs=[vm] * (len(blocks) - 1)
        + [pl.BlockSpec(memory_space=pltpu.HBM)]
        + [pl.BlockSpec(memory_space=pltpu.HBM)] * n_w
        + [vm] * (n_w if has_acc else 0),
        out_specs=[vm] * n_w,
        out_shape=[jax.ShapeDtypeStruct((rows, ch), F32)] * n_w,
        scratch_shapes=[VMEM((depth, ch), BF16)] * n_w
        + [pltpu.SemaphoreType.DMA((n_w * len(blocks) * PIECES,))]
        + [VMEM((rows, feat), BF16), pltpu.SemaphoreType.DMA],
        compiler_params=params(12),
        cost_estimate=cost(2 * rows * depth * ch * n_w, 2 * depth * ch * n_w),
    )(*blocks[:-1], far(blocks[-1]), *map(far, weights), *(accs or ()))


def held(value):
    return pltpu.with_memory_space_constraint(value, VMEM)


def mm_kernel(roles, has_acc, edge, *refs):
    n_b = len(roles)
    lhs = refs[:n_b]
    w_ref = refs[n_b]
    total = refs[n_b + 1][...] if has_acc else None
    outs = refs[n_b + 1 + has_acc :]
    feat = lhs[0].shape[1]
    for x, role in zip(lhs, roles):
        at = pl.ds(pl.multiple_of(peer(role) * feat, feat), feat)
        part = jnp.dot(x[...], w_ref[at, :], preferred_element_type=F32)
        total = part if total is None else total + part
    outs[0][...] = total.astype(outs[0].dtype)
    if edge:
        outs[1][...] = total[total.shape[0] - edge :].astype(BF16)


def edge_kernel(role, x_ref, w_ref, acc_ref, out_ref):
    rows, feat = x_ref.shape
    start = rows - out_ref.shape[0]
    at = pl.ds(pl.multiple_of(peer(role) * feat, feat), feat)
    part = jnp.dot(x_ref[start:, :], w_ref[at, :], preferred_element_type=F32)
    out_ref[...] = (acc_ref[start:, :] + part).astype(BF16)


def mm_edge(x, role, weight, acc):
    vm = pl.BlockSpec(memory_space=VMEM)
    feat, ch = x.shape[1], weight.shape[1]
    return pl.pallas_call(
        functools.partial(edge_kernel, role),
        in_specs=[vm] * 3,
        out_specs=vm,
        out_shape=jax.ShapeDtypeStruct((EDGE, ch), BF16),
        compiler_params=params(4),
        cost_estimate=cost(2 * EDGE * feat * ch, 2 * feat * ch),
    )(x, weight, acc)


def mm(blocks, roles, weight, acc, edge=0):
    rows, feat = blocks[0].shape
    ch = weight.shape[1]
    vm = pl.BlockSpec(memory_space=VMEM)
    shapes = [jax.ShapeDtypeStruct((rows, ch), BF16 if edge else F32)]
    if edge:
        shapes.append(jax.ShapeDtypeStruct((edge, ch), BF16))
    extra = () if acc is None else (acc,)
    n = len(blocks)
    return pl.pallas_call(
        functools.partial(mm_kernel, roles, len(extra), edge),
        in_specs=[vm] * (n + 1 + len(extra)),
        out_specs=[vm] * len(shapes),
        out_shape=shapes,
        compiler_params=params(5 if n > 5 else 4),
        cost_estimate=cost(2 * n * rows * feat * ch, 2 * n * feat * ch),
    )(*blocks, weight, *extra)


def convolve(pad, w_ref, b_ref, edge, rows):
    taps = w_ref.shape[0]
    total = jnp.broadcast_to(b_ref[...], (rows, b_ref.shape[1]))
    for k in range(taps):
        at = edge - taps + 1 + k
        total = total + w_ref[k : k + 1, :] * pad[at : at + rows, :]
    return (total * jax.nn.sigmoid(total)).astype(BF16)


def project(conv, pw_ref):
    return lax.dot_general(conv, pw_ref[...], (((1,), (1,)), ((), ())), preferred_element_type=F32)


def conv_kernel(x_ref, w_ref, b_ref, pw_ref, conv_ref, proj_ref, pad):
    rows, ch = x_ref.shape
    pad[0:EDGE, :] = jnp.zeros((EDGE, ch), F32)
    pad[EDGE : EDGE + rows, :] = x_ref[...].astype(F32)
    conv = convolve(pad, w_ref, b_ref, EDGE, rows)
    conv_ref[...] = conv
    proj_ref[...] = project(conv, pw_ref)


def head_kernel(split, x_ref, tail_ref, w_ref, b_ref, pw_ref, conv0_ref, proj0_ref, conv_ref, send_ref, keep_ref, pad, acc):
    rows = x_ref.shape[0]
    head = pad.shape[0] - EDGE
    pad[0:EDGE, :] = tail_ref[...].astype(F32)
    pad[EDGE:, :] = x_ref[0:head, :].astype(F32)
    conv = convolve(pad, w_ref, b_ref, EDGE, head)
    conv_ref[...] = conv0_ref[...]
    conv_ref[0:head, :] = conv
    acc[...] = proj0_ref[...]
    acc[0:head, :] = project(conv, pw_ref)
    if split:
        half = rows // 2
        core = lax.axis_index("tp") % 2
        send_ref[...] = acc[pl.ds(pl.multiple_of((1 - core) * half, half), half), :].astype(BF16)
        keep_ref[...] = acc[pl.ds(pl.multiple_of(core * half, half), half), :]
    else:
        keep_ref[...] = acc[...].astype(keep_ref.dtype)
        send_ref[...] = jnp.zeros(send_ref.shape, send_ref.dtype)


def conv_proj(x, conv_w, conv_b, proj_wt):
    rows, ch = x.shape
    wide = proj_wt.shape[0]
    vm = pl.BlockSpec(memory_space=VMEM)
    return pl.pallas_call(
        conv_kernel,
        in_specs=[vm] * 4,
        out_specs=[vm] * 2,
        out_shape=[
            jax.ShapeDtypeStruct((rows, ch), BF16),
            jax.ShapeDtypeStruct((rows, wide), F32),
        ],
        scratch_shapes=[VMEM((EDGE + rows, ch), F32)],
        compiler_params=params(6),
        cost_estimate=cost(2 * rows * ch * wide, 2 * ch * wide),
    )(x, conv_w, conv_b, proj_wt)


def conv_head(x, tail, conv_w, conv_b, proj_wt, conv0, proj0, split):
    rows, ch = x.shape
    wide = proj_wt.shape[0]
    head = min(2 * EDGE, rows)
    half = rows // 2 if split else rows
    vm = pl.BlockSpec(memory_space=VMEM)
    return pl.pallas_call(
        functools.partial(head_kernel, split),
        in_specs=[vm] * 7,
        out_specs=[vm] * 3,
        out_shape=[
            jax.ShapeDtypeStruct((rows, ch), BF16),
            jax.ShapeDtypeStruct((half if split else EDGE, wide), BF16),
            jax.ShapeDtypeStruct((half, wide), F32 if split else BF16),
        ],
        scratch_shapes=[VMEM((EDGE + head, ch), F32), VMEM((rows, wide), F32)],
        compiler_params=params(4),
        cost_estimate=cost(2 * head * ch * wide, 2 * ch * wide),
    )(x, tail, conv_w, conv_b, proj_wt, conv0, proj0)


def spread(ref, value, groups):
    count = value.shape[0]
    for j in range(groups):
        ref[pl.ds(j, count, stride=groups), :] = value[:, j * LANES : (j + 1) * LANES]


def collect(ref, count, groups):
    return jnp.concatenate([ref[pl.ds(j, count, stride=groups), :] for j in range(groups)], axis=1)


def across(ref, bc_ref, first):
    rows = bc_ref.shape[0]
    for n in range(STATE):
        ref[pl.ds(n, rows, stride=STATE), :] = jnp.broadcast_to(
            bc_ref[:, first + n : first + n + 1], (rows, LANES)
        )


def line(ref, at, groups):
    return jnp.broadcast_to(ref[pl.ds(at, 1), :], (groups, LANES))


def scan_kernel(
    split, *refs,
):
    n_p = 2 if split else 1
    parts = refs[:n_p]
    (conv_ref, sw_ref, sb_ref, decay_ref, carried_ref,
     end_ref, pack_ref, step_s, drive_s, b_ref, bc_ref,
     proj_s, nd_s, h_s) = refs[n_p:]
    rows, ch = conv_ref.shape
    groups = ch // LANES
    if split:
        half = rows // 2
        core = lax.axis_index("tp") % 2
        proj_s[pl.ds(pl.multiple_of(core * half, half), half), :] = parts[0][...].astype(F32)
        proj_s[pl.ds(pl.multiple_of((1 - core) * half, half), half), :] = parts[1][...].astype(F32)
    else:
        proj_s[...] = parts[0][...].astype(F32)
    bc_ref[...] = proj_s[:, DT_RANK:]
    across(b_ref, bc_ref, 0)
    low = proj_s[:, :DT_RANK].astype(BF16)
    pre = jnp.dot(low, sw_ref[...], preferred_element_type=F32) + sb_ref[...]
    step = jnp.maximum(pre, 0.0) + jnp.log1p(jnp.exp(-jnp.abs(pre)))
    spread(step_s, step, groups)
    spread(drive_s, step * conv_ref[...].astype(F32), groups)
    spread(nd_s, decay_ref[...] * -LOG2E, groups)
    lead = jnp.where(lax.axis_index("ctx") == 0, 1.0, 0.0)
    spread(h_s, carried_ref[...] * lead, groups)
    nd = [nd_s[n * groups : (n + 1) * groups, :] for n in range(STATE)]
    h0 = tuple(h_s[n * groups : (n + 1) * groups, :] for n in range(STATE))

    def body(t, carry):
        h, total = carry
        at = pl.ds(pl.multiple_of(t * groups, groups), groups)
        dt = step_s[at, :]
        u = drive_s[at, :]
        new = tuple(
            jnp.exp2(dt * nd[n]) * h[n] + u * line(b_ref, t * STATE + n, groups)
            for n in range(STATE)
        )
        return new, total + dt

    h, total = lax.fori_loop(0, rows, body, (h0, jnp.zeros((groups, LANES), F32)), unroll=8)
    for n in range(STATE):
        h_s[n * groups : (n + 1) * groups, :] = h[n]
    end_ref[0:STATE, :] = collect(h_s, STATE, groups)
    nd_s[0:groups, :] = total
    end_ref[STATE : STATE + 1, :] = collect(nd_s, 1, groups)
    pack_ref[...] = end_ref[...].astype(BF16)


def scan(parts, conv_x, step_w, step_b, decay_t, carried_t):
    rows, ch = conv_x.shape
    groups = ch // LANES
    vm = pl.BlockSpec(memory_space=VMEM)
    return pl.pallas_call(
        functools.partial(scan_kernel, len(parts) == 2),
        in_specs=[vm] * (5 + len(parts)),
        out_specs=[vm] * 6,
        out_shape=[
            jax.ShapeDtypeStruct((STATE + 1, ch), F32),
            jax.ShapeDtypeStruct((STATE + 1, ch), BF16),
            jax.ShapeDtypeStruct((rows * groups, LANES), F32),
            jax.ShapeDtypeStruct((rows * groups, LANES), F32),
            jax.ShapeDtypeStruct((rows * STATE, LANES), F32),
            jax.ShapeDtypeStruct((rows, 2 * STATE), F32),
        ],
        scratch_shapes=[
            VMEM((rows, parts[0].shape[1]), F32),
            VMEM((STATE * groups, LANES), F32),
            VMEM((STATE * groups, LANES), F32),
        ],
        compiler_params=params(8),
        cost_estimate=cost(rows * ch * STATE * 8, rows * ch * 8, rows * ch * STATE),
    )(*parts, conv_x, step_w, step_b, decay_t, carried_t)


def local_kernel(step_ref, drive_ref, b_ref, bc_ref, decay_ref, carried_ref, y_ref, cum_ref, c_ref, nd_s, h_s):
    across(c_ref, bc_ref, STATE)
    groups = decay_ref.shape[1] // LANES
    rows = step_ref.shape[0] // groups
    spread(nd_s, decay_ref[...] * -LOG2E, groups)
    lead = jnp.where(lax.axis_index("ctx") == 0, 1.0, 0.0)
    spread(h_s, carried_ref[...] * lead, groups)
    nd = [nd_s[n * groups : (n + 1) * groups, :] for n in range(STATE)]
    h0 = tuple(h_s[n * groups : (n + 1) * groups, :] for n in range(STATE))

    def body(t, carry):
        h, total = carry
        at = pl.ds(pl.multiple_of(t * groups, groups), groups)
        dt = step_ref[at, :]
        u = drive_ref[at, :]
        total = total + dt
        cum_ref[at, :] = total
        y = None
        new = []
        for n in range(STATE):
            v = jnp.exp2(dt * nd[n]) * h[n] + u * line(b_ref, t * STATE + n, groups)
            new.append(v)
            term = v * line(c_ref, t * STATE + n, groups)
            y = term if y is None else y + term
        y_ref[at, :] = y
        return tuple(new), total

    lax.fori_loop(0, rows, body, (h0, jnp.zeros((groups, LANES), F32)), unroll=8)


def local_readout(step, drive, b, bc, decay_t, carried_t):
    groups = decay_t.shape[1] // LANES
    vm = pl.BlockSpec(memory_space=VMEM)
    return pl.pallas_call(
        local_kernel,
        in_specs=[vm] * 6,
        out_specs=[vm] * 3,
        out_shape=[jax.ShapeDtypeStruct(step.shape, F32)] * 2
        + [jax.ShapeDtypeStruct(b.shape, F32)],
        scratch_shapes=[VMEM((STATE * groups, LANES), F32)] * 2,
        compiler_params=params(4),
        cost_estimate=cost(step.size * STATE * 8, step.size * 16, step.size * STATE),
    )(step, drive, b, bc, decay_t, carried_t)


def weight_kernel(cum_ref, c_ref, decay_ref, q_ref, nd_s):
    groups = decay_ref.shape[1] // LANES
    rows = cum_ref.shape[0] // groups
    spread(nd_s, decay_ref[...] * -LOG2E, groups)
    nd = [nd_s[n * groups : (n + 1) * groups, :] for n in range(STATE)]

    def body(t, carry):
        total = cum_ref[pl.ds(pl.multiple_of(t * groups, groups), groups), :]
        for n in range(STATE):
            at = pl.ds(pl.multiple_of((t * STATE + n) * groups, groups), groups)
            q_ref[at, :] = jnp.exp2(total * nd[n]) * line(c_ref, t * STATE + n, groups)
        return carry

    lax.fori_loop(0, rows, body, 0, unroll=4)


def weights(cum, c, decay_t):
    groups = decay_t.shape[1] // LANES
    vm = pl.BlockSpec(memory_space=VMEM)
    return pl.pallas_call(
        weight_kernel,
        in_specs=[vm] * 3,
        out_specs=vm,
        out_shape=jax.ShapeDtypeStruct((cum.shape[0] * STATE, LANES), F32),
        scratch_shapes=[VMEM((STATE * groups, LANES), F32)],
        compiler_params=params(2),
        cost_estimate=cost(cum.size * STATE * 3, cum.size * 4, cum.size * STATE),
    )(cum, c, decay_t)


def add_kernel(*refs):
    total = refs[0][...].astype(F32)
    for r in refs[1:-1]:
        total = total + r[...].astype(F32)
    refs[-1][...] = total.astype(BF16)


def add(*values):
    vm = pl.BlockSpec(memory_space=VMEM)
    shape = values[0].shape
    size = shape[0] * shape[1]
    return pl.pallas_call(
        add_kernel,
        in_specs=[vm] * len(values),
        out_specs=vm,
        out_shape=jax.ShapeDtypeStruct(shape, BF16),
        compiler_params=params(3),
        cost_estimate=cost(size * len(values), 2 * size * len(values)),
    )(*values)


def add_pair_kernel(a_ref, b_ref, *outs):
    for i, o in enumerate(outs):
        o[...] = (a_ref[i].astype(F32) + b_ref[i].astype(F32)).astype(BF16)


def add_pair(a, b):
    vm = pl.BlockSpec(memory_space=VMEM)
    n, rows, feat = a.shape
    return pl.pallas_call(
        add_pair_kernel,
        in_specs=[vm, vm],
        out_specs=[vm] * n,
        out_shape=[jax.ShapeDtypeStruct((rows, feat), BF16)] * n,
        compiler_params=params(3),
        cost_estimate=cost(a.size, 6 * a.size),
    )(a, b)


def merge_kernel(bit, first, last, decay_ref, group_ref, got_ref, *refs):
    ent_ref = None if first else refs[0]
    pack_ref, out_ref = refs[-2:]
    upper = (lax.axis_index("ctx") // bit) % 2 == 1
    decay = decay_ref[...]
    got = got_ref[...].astype(F32)
    gh, gs = got[:STATE], got[STATE:]
    mh, ms = group_ref[:STATE, :], group_ref[STATE:, :]
    entering = gh if first else jnp.exp(-decay * ent_ref[STATE:, :]) * gh + ent_ref[:STATE, :]
    before = gs if first else ent_ref[STATE:, :] + gs
    keep_h = jnp.zeros_like(gh) if first else ent_ref[:STATE, :]
    keep_s = jnp.zeros_like(gs) if first else ent_ref[STATE:, :]
    out_ref[:STATE, :] = jnp.where(upper, entering, keep_h)
    out_ref[STATE:, :] = jnp.where(upper, before, keep_s)
    low = jnp.where(upper, gh, mh)
    high = jnp.where(upper, mh, gh)
    high_s = jnp.where(upper, ms, gs)
    total = jnp.exp(-decay * high_s) * low + high
    pack_ref[:STATE, :] = total.astype(BF16)
    if not last:
        pack_ref[STATE:, :] = (ms + gs).astype(BF16)
        refs[-3][:STATE, :] = total
        refs[-3][STATE:, :] = ms + gs


def merge(bit, decay_t, group, got, ent, last):
    vm = pl.BlockSpec(memory_space=VMEM)
    first = ent is None
    extra = () if first else (ent,)
    return pl.pallas_call(
        functools.partial(merge_kernel, bit, first, last),
        in_specs=[vm] * (3 + len(extra)),
        out_specs=[vm] * (2 if last else 3),
        out_shape=[jax.ShapeDtypeStruct(group.shape, F32)] * (not last)
        + [
            jax.ShapeDtypeStruct((STATE + (not last), group.shape[1]), BF16),
            jax.ShapeDtypeStruct(group.shape, F32),
        ],
        compiler_params=params(3),
        cost_estimate=cost(group.size * 8, group.size * 16),
    )(decay_t, group, got, *extra)


def gate_kernel(bit, first, y_ref, q_ref, end_ref, got_ref, decay_ref, conv_ref, skip_ref, gate_ref, *refs):
    ent_ref = None if first else refs[0]
    out_ref, bound_ref, e_s, y_s = refs[-4:]
    rows, ch = conv_ref.shape
    groups = ch // LANES
    decay = decay_ref[...]
    upper = (lax.axis_index("ctx") // bit) % 2 == 1
    got = got_ref[...].astype(F32)[:STATE]
    if first:
        entering = jnp.where(upper, got, jnp.zeros_like(got))
    else:
        kept = ent_ref[:STATE, :]
        entering = jnp.where(upper, jnp.exp(-decay * ent_ref[STATE:, :]) * got + kept, kept)
    bound_ref[...] = jnp.exp(-decay * end_ref[STATE:, :]) * entering + end_ref[:STATE, :]
    spread(e_s, entering, groups)
    ent = [e_s[n * groups : (n + 1) * groups, :] for n in range(STATE)]

    def body(t, carry):
        at = pl.ds(pl.multiple_of(t * groups, groups), groups)
        y = y_ref[at, :]
        for n in range(STATE):
            y = y + q_ref[pl.ds(pl.multiple_of((t * STATE + n) * groups, groups), groups), :] * ent[n]
        y_s[at, :] = y
        return carry

    lax.fori_loop(0, rows, body, 0, unroll=8)
    y = collect(y_s, rows, groups)
    gate = gate_ref[...].astype(BF16).astype(F32)
    out = (y + skip_ref[...] * conv_ref[...].astype(F32)) * (gate * jax.nn.sigmoid(gate))
    out_ref[...] = out.astype(BF16)


def gating(bit, y, q, end, got, ent, decay_t, conv_x, skip, gate):
    rows, ch = conv_x.shape
    groups = ch // LANES
    vm = pl.BlockSpec(memory_space=VMEM)
    first = ent is None
    extra = () if first else (ent,)
    return pl.pallas_call(
        functools.partial(gate_kernel, bit, first),
        in_specs=[vm] * (8 + len(extra)),
        out_specs=[vm, vm],
        out_shape=[
            jax.ShapeDtypeStruct((rows, ch), BF16),
            jax.ShapeDtypeStruct((STATE, ch), F32),
        ],
        scratch_shapes=[
            VMEM((STATE * groups, LANES), F32),
            VMEM((rows * groups, LANES), F32),
        ],
        compiler_params=params(8),
        cost_estimate=cost(rows * ch * STATE * 6, rows * ch * 8, rows * ch * STATE),
    )(y, q, end, got, decay_t, conv_x, skip, gate, *extra)


def out_stack_kernel(masks, g_ref, w_ref, out):
    feat = out.shape[2]
    for i, mask in enumerate(masks):
        at = pl.ds(pl.multiple_of(peer(mask) * feat, feat), feat)
        out[i] = jnp.dot(g_ref[...], w_ref[:, at], preferred_element_type=F32).astype(BF16)


def out_blocks(gated, weight, masks, feat):
    rows, ch = gated.shape
    n = len(masks)
    vm = pl.BlockSpec(memory_space=VMEM)
    return pl.pallas_call(
        functools.partial(out_stack_kernel, masks),
        in_specs=[vm, vm],
        out_specs=vm,
        out_shape=jax.ShapeDtypeStruct((n, rows, feat), BF16),
        compiler_params=params(4),
        cost_estimate=cost(2 * rows * ch * feat * n, 2 * ch * feat * n),
    )(gated, weight)


def on_device(
    tokens, inner_weight, gate_weight, conv_weight, conv_bias, proj_weight, step_weight,
    step_bias, decay_rate, skip_gain, out_weight, carried_state,
):
    rows, feat = tokens.shape
    n_tp = lax.axis_size("tp")
    n_ctx = lax.axis_size("ctx")
    square = n_tp == 8
    shift = [(i, i + 1) for i in range(n_ctx - 1)]
    proj_wt = proj_weight.T
    decay_t = decay_rate.T
    carried_t = carried_state.T

    if square:
        to_first = [(i, i ^ (2 + 2 * (i % 2))) for i in range(n_tp)]
        to_second = [(i, i ^ (4 - 2 * (i % 2))) for i in range(n_tp)]
        p1 = flip(tokens, "tp", 1)
        vs = lax.ppermute(tokens, "tp", to_second)
        inner, = stream_mm([tokens], [0], [inner_weight], None)
        vf = lax.ppermute(tie(tokens, inner), "tp", to_first)
        vs = tie(vs, inner)
        vd = lax.ppermute(vs, "tp", to_first)
        qs = flip(vs, "tp", 1)
        qf = flip(vf, "tp", 1)
        inner_w, gate_w = held(inner_weight), held(gate_weight)
        inner, = mm([p1, vs, qs, vf, qf], [1, 20, 11, 10, 21], inner_w, inner)
        vd = tie(vd, inner)
        qd = flip(vd, "tp", 1)
        inner, = mm([vd], [6], inner_w, inner)
        qd = tie(qd, inner)
        edge_x = mm_edge(qd, 7, inner_w, inner)
        inner_x, _ = mm([qd], [7], inner_w, inner, EDGE)
    else:
        piece = lax.all_gather(tokens, "tp", axis=1, tiled=True)
        inner_x = jnp.dot(piece, inner_weight, preferred_element_type=F32).astype(BF16)
        gate_acc = jnp.dot(piece, gate_weight, preferred_element_type=F32)
        edge_x = inner_x[rows - EDGE :]

    tail = lax.ppermute(edge_x, "ctx", shift)
    conv_b = conv_bias[None, :]
    conv0, proj0 = conv_proj(inner_x, conv_weight, conv_b, proj_wt)
    conv_x, send, keep = conv_head(
        inner_x, tie(tail, proj0), conv_weight, conv_b, proj_wt, conv0, proj0, square
    )
    if square:
        part = add(keep, flip(send, "tp", 1))
        quarter = [flip(part, "tp", m) for m in (2, 4, 6)]
        blocks = [tokens, p1, vs, qs, vf, qf, vd, qd]
        gate_acc, = mm(
            [tie(tokens, part), *blocks[1:]], [0, 1, 20, 11, 10, 21, 6, 7], gate_w, None
        )
        quarter = [tie(v, gate_acc) for v in quarter]
        mine = add(part, *quarter)
        parts = (mine, flip(mine, "tp", 1))
    else:
        parts = (lax.psum(keep, "tp"),)
    end, packet, step, drive, b_rows, bc = scan(
        parts, conv_x, step_weight, step_bias[None, :], decay_t, carried_t
    )

    y, cum, c_rows = local_readout(step, drive, b_rows, bc, decay_t, carried_t)
    group, ent, bit = end, None, 1
    while bit * 2 < n_ctx:
        got = flip(packet, "ctx", bit)
        if bit == 1:
            got = tie(got, y)
        *group, packet, ent = merge(bit, decay_t, group, got, ent, bit * 4 >= n_ctx)
        group = group[0] if group else None
        bit *= 2
    got = flip(packet, "ctx", bit)
    q = weights(cum, c_rows, tie(decay_t, packet))
    got = tie(got, q)
    gated, bound = gating(
        bit, y, q, end, got, ent, decay_t, conv_x, skip_gain[None, :], gate_acc
    )
    if square:
        out_weight = pltpu.with_memory_space_constraint(out_weight, VMEM)
        away = out_blocks(gated, out_weight, [7, 21], feat)
        got = flip(away, "tp", 1)
        away_b = out_blocks(gated, out_weight, [11, 1], feat)
        got_b = flip(away_b, "tp", 1)
        near = out_blocks(gated, out_weight, [6, 10], feat)
        sd, sf = add_pair(near, got)
        near_b = out_blocks(gated, out_weight, [20, 0], feat)
        ss, so = add_pair(near_b, got_b)
        rd = lax.ppermute(sd, "tp", to_first)
        rf = lax.ppermute(sf, "tp", to_first)
        rs = lax.ppermute(add(ss, rd), "tp", to_second)
        mixed = add(so, rf, rs)
    else:
        partial = jnp.dot(gated, out_weight, preferred_element_type=F32).astype(BF16)
        mixed = lax.psum_scatter(partial, "tp", scatter_dimension=1, tiled=True)
    return (mixed, bound.T[None])


def solution(mesh):
    in_specs = (
        P("ctx", "tp"), P(None, "tp"), P(None, "tp"), P(None, "tp"), P("tp"), P("tp", None),
        P(None, "tp"), P("tp"), P("tp", None), P("tp"), P("tp", None), P("tp", None),
    )
    out_specs = (P("ctx", "tp"), P("ctx", "tp", None))
    return jax.shard_map(
        on_device, mesh=mesh, in_specs=in_specs, out_specs=out_specs, check_vma=False
    )
```
